128 devices in a mesh: blk: 8 (over z, y_hi), slab: 16 (over x, y_lo, core).
Axes of the slice: x: 4, y: 4 (y_hi: 2, y_lo: 2; y = y_hi * 2 + y_lo), z: 4, core: 2. Of those that a mesh axis runs over, the one named last changes fastest.
Arguments:
- new_rows: bfloat16 [65536, 768], P(('blk', 'slab')), may hold values from -6 to 6
- index_rows: bfloat16 [32768, 768], P('blk'), may hold values from -6 to 6
- pattern: int32 [128, 8], replicated, may hold values from 0 to 1, as said below
- kept_row: int32 [32768], P(('blk', 'slab')), may hold values from 0 to 511
- kept_owner: int32 [32768, 1], P(('blk', 'slab')), may hold values from 0 to 127; in each aligned block of 256 rows (0 to 255, 256 to 511, ...) at most 4 rows name the same one
- kept_local: int32 [32768], P(('blk', 'slab')), may hold values from 0 to 15
Outputs:
- best_cosine: float32 [65536], P(('blk', 'slab'))
- centroid_sums: float32 [2048, 768], P(('blk', 'slab'))
- kept_counts: float32 [2048], P(('blk', 'slab'))
The draws below stay inside these ranges and needn't reach their ends.
Inputs may be any that keep to these rules, and one draw needn't show every extreme that they name: `pattern`: every row has at least one 1. `kept_owner`: the 256 entries of one device name one owner at most 4 times, a bound that some block reaches.
All inputs are finite; a program needn't handle non-finite values.
Results may differ from the reference program's by a relative error of at most 0.0029.
Values may be sent and summed in bfloat16 or wider, within the bound.
A program may use at most 64 MiB of HBM per device.

```python
import math
import jax
import jax.numpy as jnp
import numpy as np
from jax import lax

D = 768
NEW_DEV = 512
IDX_BLK = 4096
KEEP_DEV = 256
CL_DEV = 16
KCAP = 4
NEW_BLOCKS = 128
IDX_BLOCKS = 8
NEW = 65536
IDX = 32768
NCLUS = 2048
KEEP = 32768
DEVICES = 128


def draw_pattern(key, part):
    key_level, key_noise, key_pick = jax.random.split(jax.random.fold_in(key, 17), 3)
    level = jax.random.randint(key_level, (NEW_BLOCKS, 1), 1, IDX_BLOCKS + 1)
    noise = jax.random.randint(key_noise, (NEW_BLOCKS, IDX_BLOCKS), 0, IDX_BLOCKS)
    chosen = jax.random.randint(key_pick, (NEW_BLOCKS, 1), 0, IDX_BLOCKS)
    columns = jnp.arange(IDX_BLOCKS, dtype=jnp.int32)[None, :]
    return ((noise < level) | (columns == chosen)).astype(jnp.int32)


def place_ends(values, stream_key, low, largest):
    longest = values.shape.index(max(values.shape))
    spots = []
    for shift in (0, 1):
        where = [jax.random.randint(jax.random.fold_in(stream_key, axis), (), 0, length) for axis, length in enumerate(values.shape)]
        where[longest] = (where[longest] + shift) % values.shape[longest]
        spots.append(tuple(where))
    return values.at[spots[0]].set(low).at[spots[1]].set(largest)


def block_levels(key, dims, shards, low, top_value):
    def one(position, parts):
        draws = jax.random.uniform(jax.random.fold_in(jax.random.fold_in(key, 6), position), (parts,), jnp.float32, low / len(shards), top_value / len(shards))
        return jnp.repeat(jnp.exp(draws), dims[position] // parts).reshape((-1,) + (1,) * (len(dims) - position - 1))

    factor_of = one(*shards[0])
    for cut in shards[1:]:
        factor_of = factor_of * one(*cut)
    return factor_of


def deal_out(rng, own, number, rows, amount, top, bound, skew):
    ranking = jax.random.permutation(rng, amount)
    crowded, ordinary = load_shares(amount, rows * top, bound, skew, True), load_shares(amount, rows * top, bound, skew, False)
    places = jnp.arange(amount)

    def named(sizes, rotation):
        used = int((sizes > 0).sum())
        fixed = max(1, used // 4)
        shifted = fixed + (places - fixed + rotation * (used - fixed)) % max(1, amount - fixed)
        return jnp.zeros((amount,), jnp.int32).at[ranking[jnp.where(places < fixed, places, shifted)]].set(jnp.asarray(sizes, jnp.int32))

    sizes = jnp.where(number % 4 == 0, named(crowded, number // 4), named(ordinary, number - number // 4 - 1))
    mixed = jax.random.permutation(jax.random.fold_in(own, 3), amount)
    giver, taker = mixed[0:amount // 2 * 2:2], mixed[1:amount // 2 * 2:2]
    margin = jnp.minimum(sizes[giver] - 1, bound - sizes[taker]) // 2
    margin = jnp.where((giver == ranking[0]) | (taker == ranking[0]) | (sizes[taker] == 0), 0, jnp.maximum(margin, 0))
    shifted = jax.random.randint(jax.random.fold_in(own, 4), (amount // 2,), 0, 1 << 20) % (margin + 1)
    sizes = sizes.at[giver].add(-shifted).at[taker].add(shifted)
    members = jnp.searchsorted(jnp.cumsum(sizes), jnp.arange(rows * top), side="right").astype(jnp.int32)
    table = members.reshape(top, rows).T
    table = table[jax.random.permutation(jax.random.fold_in(own, 1), rows)]
    rotation = jax.random.randint(jax.random.fold_in(own, 2), (rows, 1), 0, top)
    return jnp.take_along_axis(table, (jnp.arange(top)[None, :] + rotation) % top, axis=1)


def load_shares(amount, total, bound, lean, full):
    weights = [(1 << 20) // math.isqrt(standing ** lean) + 1 for standing in range(1, amount + 1)]
    largest = bound if full else min(bound, max(-(-total // amount), total * weights[0] // sum(weights)))
    least = 1 if total - largest >= amount - 1 else 0
    holding, spare = [largest] + [least] * (amount - 1), total - largest - least * (amount - 1)
    while spare > 0:
        free = [i for i in range(1, amount) if holding[i] < largest] or [i for i in range(1, amount) if holding[i] < bound]
        whole, left = sum([weights[i] for i in free]), spare
        for i in free:
            more = min(bound - holding[i], max(1, left * weights[i] // whole), spare)
            holding[i] = holding[i] + more
            spare = spare - more
    return np.array(holding)


def bell_draw(key, dims, spread, reach, pieces=(), kind=jnp.bfloat16):
    values = jax.random.normal(key, dims, jnp.float32) * spread
    if len(pieces) > 0:
        values = block_levels(key, dims, pieces, -0.22, 0.18) * values
    return jnp.clip(values, min=-reach, max=reach).astype(kind)


def setup_inputs(seed: int = 0) -> dict:
    arg_keys = jax.random.split(jax.random.key(seed), 7)
    new_rows = bell_draw(arg_keys[0], (NEW, D), 1.0, 6.0, ((0, 128),))
    index_rows = bell_draw(arg_keys[1], (IDX, D), 1.0, 6.0, ((0, 8),))
    pattern = draw_pattern(jax.random.fold_in(arg_keys[6], 71), 0)
    kept_row = place_ends(jax.random.randint(arg_keys[3], (KEEP,), 0, NEW_DEV), jax.random.fold_in(arg_keys[3], 1), 0, NEW_DEV - 1).astype(jnp.int32)
    kept_owner_keys = jax.random.split(jax.random.fold_in(arg_keys[4], 1), KEEP // KEEP_DEV)
    kept_owner_turns = jax.random.permutation(jax.random.fold_in(arg_keys[4], 3), KEEP // KEEP_DEV)
    kept_owner = jax.vmap(lambda own, number: deal_out(jax.random.fold_in(arg_keys[4], 2), own, number, KEEP_DEV, DEVICES, 1, KCAP, 2))(kept_owner_keys, kept_owner_turns).reshape((KEEP, 1))
    kept_local = place_ends(jax.random.randint(arg_keys[5], (KEEP,), 0, CL_DEV), jax.random.fold_in(arg_keys[5], 1), 0, CL_DEV - 1).astype(jnp.int32)
    return {"new_rows": new_rows, "index_rows": index_rows, "pattern": pattern, "kept_row": kept_row, "kept_owner": kept_owner, "kept_local": kept_local}


EPS = 1e-06

def unit_rows(values):
    wide = values.astype(jnp.float32)
    scale = lax.rsqrt(lax.optimization_barrier(jnp.sum(wide * wide, axis=-1, keepdims=True)) + EPS)
    return (wide * scale).astype(jnp.bfloat16)

def reference(new_rows, index_rows, pattern, kept_row, kept_owner, kept_local):
    new_unit = unit_rows(new_rows)
    index_unit = unit_rows(index_rows)
    blocks = new_unit.reshape(NEW_BLOCKS, NEW_DEV, D)
    col_block = jnp.arange(IDX, dtype=jnp.int32) // IDX_BLK

    def block_max(args):
        rows, marks = args
        scores = lax.dot_general(rows, index_unit, (((1,), (1,)), ((), ())), preferred_element_type=jnp.float32)
        live = marks[col_block] > 0
        masked = jnp.where(live[None, :], scores, jnp.float32(-2.0))
        return lax.optimization_barrier(jnp.max(masked, axis=1))
    best = lax.map(block_max, (blocks, pattern)).reshape(NEW)
    entry = jnp.arange(KEEP, dtype=jnp.int32)
    global_row = entry // KEEP_DEV * NEW_DEV + kept_row.astype(jnp.int32)
    picked = new_unit[global_row].astype(jnp.float32)
    cluster = (kept_owner[:, 0] * CL_DEV + kept_local).astype(jnp.int32)
    sums = jax.ops.segment_sum(picked, cluster, num_segments=NCLUS)
    counts = jax.ops.segment_sum(jnp.ones((KEEP,), jnp.float32), cluster, num_segments=NCLUS)
    return (best, sums, counts)
```

```python
import functools

import jax
import jax.numpy as jnp
from jax import lax
from jax.experimental import pallas as pl
from jax.experimental.pallas import tpu as pltpu
from jax.sharding import PartitionSpec as P

CL_DEV = 16
EPS = 1e-06
MESH = pl.DeviceIdType.MESH
ROWS = 512
CH = 128
D = 768
HALF = 2048


def sent_together(arrays, axis, split_dim, concat_dim, along):
    both = jnp.concatenate(arrays, axis=along)
    out, at, done = (
        lax.all_to_all(both, axis, split_axis=split_dim, concat_axis=concat_dim, tiled=True),
        0,
        [],
    )
    for a in arrays:
        done.append(lax.slice_in_dim(out, at, at + a.shape[along], axis=along))
        at += a.shape[along]
    return tuple(done)


def unit_rows(values):
    wide = values.astype(jnp.float32)
    scale = lax.rsqrt(jnp.sum(wide * wide, axis=-1, keepdims=True) + EPS)
    return (wide * scale).astype(jnp.bfloat16)


def ring4(v):
    return lax.rem(v + 4, 4)


def quad_at(k):
    return 2 * ROWS + ROWS * k


CROSS_AT = (0, 1, 4, 5)
XM_AT = (2, 6, 8, 10)
XP_AT = (3, 7, 9, 11)
X2_AT = (12, 13, 14, 15)


def best_kernel(
    new_hbm, index_hbm, pattern, out_ref,
    nr, ir, oi, acc0, acc1, ret_out, ret_in,
    load_sem, bar_unused,
    z_s, z_r, z2_s, z2_r, sib_s, sib_r, cr_s, cr_r, x_s, x_r, x2_s, x2_r, ret_s, ret_r,
):
    b = lax.axis_index("blk")
    s = lax.axis_index("slab")
    z, h = lax.div(b, 2), lax.rem(b, 2)
    x, l, c = lax.div(s, 4), lax.rem(lax.div(s, 2), 2), lax.rem(s, 2)

    def blk_of(dz, dh=0):
        return ring4(z + dz) * 2 + (1 - h if dh else h)

    def slab_of(dx=0, dl=0, dc=0):
        return (ring4(x + dx) * 2 + (1 - l if dl else l)) * 2 + (1 - c if dc else c)

    zp, zm = (blk_of(1), s), (blk_of(-1), s)
    xp, xm = (b, slab_of(1)), (b, slab_of(-1))
    sib = (b, slab_of(0, 0, 1))
    cross = (blk_of(0, 1), slab_of(0, 1, 0))
    back = [(dz, dc) for dz in (0, 1, 2, 3) for dc in (0, 1) if (dz, dc) != (0, 0)]
    back_id = [(blk_of(dz), slab_of(0, 0, dc)) for dz, dc in back]
    partners = [xp, xm, cross] + back_id

    barrier = pltpu.get_barrier_semaphore()
    for p in partners:
        pl.semaphore_signal(barrier, inc=1, device_id=p, device_id_type=MESH)

    load_new = pltpu.make_async_copy(new_hbm, nr.at[pl.ds(0, ROWS)], load_sem.at[0])
    load_new.start()
    loads = []
    for j in range(4):
        u = ring4(x + j)
        at = pl.multiple_of(u * ROWS, ROWS)
        cp = pltpu.make_async_copy(
            index_hbm.at[pl.ds(pl.multiple_of(c * HALF + u * ROWS, ROWS), ROWS)],
            ir.at[pl.ds(at, ROWS)],
            load_sem.at[1 + j],
        )
        cp.start()
        loads.append((cp, at))

    def remote(src, dst, ss, rs, dev):
        return pltpu.make_async_remote_copy(
            src_ref=src, dst_ref=dst, send_sem=ss, recv_sem=rs, device_id=dev, device_id_type=MESH
        )

    def rows(ref, at, n=CH):
        return ref.at[pl.ds(at, n)]

    own_p = [remote(rows(nr, CH * k), rows(nr, quad_at(k)), z_s.at[0, k], z_r.at[0, k], zp) for k in range(4)]
    own_m = [
        remote(rows(nr, CH * ((k + 2) % 4)), rows(nr, quad_at(k) + CH), z_s.at[1, k], z_r.at[1, k], zm)
        for k in range(4)
    ]
    fwd_p = [remote(rows(nr, quad_at(k)), rows(nr, quad_at(4 + k)), z2_s.at[0, k], z2_r.at[0, k], zp) for k in range(2)]
    fwd_m = [
        remote(rows(nr, quad_at(k) + CH), rows(nr, quad_at(4 + k) + CH), z2_s.at[1, k], z2_r.at[1, k], zm)
        for k in range(2)
    ]
    to_sib = [remote(rows(nr, 0, ROWS), rows(nr, ROWS, ROWS), sib_s.at[6], sib_r.at[6], sib)]
    pair_sib = [
        remote(rows(nr, quad_at(k), 2 * CH), rows(nr, quad_at(k) + 2 * CH, 2 * CH), sib_s.at[k], sib_r.at[k], sib)
        for k in range(6)
    ]
    cr = [
        remote(
            ir.at[pl.ds(pl.multiple_of(x * ROWS + CH * k, CH), CH)],
            rows(oi, CH * CROSS_AT[k]), cr_s.at[k], cr_r.at[k], cross,
        )
        for k in range(4)
    ]
    x_p = [remote(rows(oi, CH * CROSS_AT[k]), rows(oi, CH * XM_AT[k]), x_s.at[0, k], x_r.at[0, k], xp) for k in range(4)]
    x_m = [remote(rows(oi, CH * CROSS_AT[k]), rows(oi, CH * XP_AT[k]), x_s.at[1, k], x_r.at[1, k], xm) for k in range(4)]
    x_f = [
        remote(rows(oi, CH * XM_AT[k]), rows(oi, CH * X2_AT[k]), x2_s.at[k], x2_r.at[k], xp)
        if k % 2 == 0
        else remote(rows(oi, CH * XP_AT[k]), rows(oi, CH * X2_AT[k]), x2_s.at[k], x2_r.at[k], xm)
        for k in range(4)
    ]

    acc0[...] = jnp.full(acc0.shape, -3.0, jnp.float32)
    acc1[...] = jnp.full(acc1.shape, -3.0, jnp.float32)

    def normalize(ref, at, n=CH):
        ref[pl.ds(at, n), :] = unit_rows(ref[pl.ds(at, n), :])

    load_new.wait()
    normalize(nr, 0)
    normalize(nr, 2 * CH)
    pl.semaphore_wait(barrier, len(partners))
    own_p[0].start()
    own_m[0].start()
    normalize(nr, CH)
    normalize(nr, 3 * CH)
    for k in range(1, 4):
        own_p[k].start()
        own_m[k].start()
    to_sib[0].start()

    loads[0][0].wait()
    for k in range(4):
        normalize(ir, pl.multiple_of(x * ROWS + CH * k, CH))
        cr[k].start()
    for cp, at in loads[1:]:
        cp.wait()
        for k in range(4):
            normalize(ir, pl.multiple_of(at + CH * k, CH))

    def scores(acc, idx, i_at, i_n, n_at, n_n):
        prod = lax.dot_general(
            idx[pl.ds(i_at, i_n), :], nr[pl.ds(n_at, n_n), :],
            (((1,), (1,)), ((), ())), preferred_element_type=jnp.float32,
        )
        top = jnp.max(prod.reshape(i_n // 8, 8, n_n), axis=0)
        acc[:, pl.ds(n_at, n_n)] = jnp.maximum(acc[:, pl.ds(n_at, n_n)], top)

    def own_range(n_at):
        scores(acc0, ir, 0, HALF, n_at, ROWS)

    def other_range(g, half):
        scores(acc1, oi, ROWS * g, ROWS, HALF * half, HALF)

    own_range(0)
    to_sib[0].wait_recv()
    own_range(ROWS)

    def z_in(k):
        if k < 4:
            own_p[k].wait_recv()
            if k < 2:
                fwd_p[k].start()
            own_m[k].wait_recv()
            if k < 2:
                fwd_m[k].start()
        else:
            fwd_p[k - 4].wait_recv()
            fwd_m[k - 4].wait_recv()
        pair_sib[k].start()

    def cross_in(k):
        cr[k].wait_recv()
        x_p[k].start()
        x_m[k].start()

    def x_in(k):
        x_p[k].wait_recv()
        if k % 2 == 0:
            x_f[k].start()
        x_m[k].wait_recv()
        if k % 2 == 1:
            x_f[k].start()

    def quad(k):
        pair_sib[k].wait_recv()
        own_range(quad_at(k))

    z_in(0)
    cross_in(0)
    quad(0)
    z_in(1)
    cross_in(1)
    x_in(0)
    quad(1)
    z_in(2)
    cross_in(2)
    x_in(1)
    quad(2)
    other_range(0, 0)
    z_in(3)
    cross_in(3)
    quad(3)
    x_in(2)
    other_range(1, 0)
    z_in(4)
    x_in(3)
    quad(4)
    other_range(2, 0)
    z_in(5)
    quad(5)
    other_range(0, 1)
    other_range(1, 1)
    other_range(2, 1)
    for k in range(4):
        x_f[k].wait_recv()
    other_range(3, 0)
    other_range(3, 1)

    def block_best(dz, dc):
        side = 2 * CH * dc
        if dz == 0:
            where = [ROWS * dc + CH * q for q in range(4)]
        elif dz == 3:
            where = [quad_at(q) + side for q in range(4)]
        elif dz == 1:
            where = [quad_at((q + 2) % 4) + side + CH for q in range(4)]
        else:
            where = [quad_at(4 + q % 2) + side + CH * (q // 2) for q in range(4)]
        row = blk_of(dz) * 16 + slab_of(0, 0, dc)
        live0 = jnp.full((1, ROWS), pattern[row, b], jnp.int32) > 0
        live1 = jnp.full((1, ROWS), pattern[row, blk_of(0, 1)], jnp.int32) > 0

        def top(acc):
            parts = [jnp.max(acc[:, pl.ds(w, CH)], axis=0, keepdims=True) for w in where]
            return jnp.concatenate(parts, axis=1)

        return jnp.maximum(jnp.where(live0, top(acc0), -2.0), jnp.where(live1, top(acc1), -2.0))

    rets = []
    for i, (dz, dc) in enumerate(back):
        ret_out[i] = block_best(dz, dc)
        cp = remote(ret_out.at[i], ret_in.at[i], ret_s.at[i], ret_r.at[i], back_id[i])
        cp.start()
        rets.append(cp)
    best = block_best(0, 0)
    for cp in rets:
        cp.wait_recv()
    for i in range(len(back)):
        best = jnp.maximum(best, ret_in[i])
    out_ref[...] = best
    for cp in own_p + own_m + fwd_p + fwd_m + to_sib + pair_sib + cr + x_p + x_m + x_f + rets:
        cp.wait_send()


def best_of(new_rows, index_rows, pattern):
    dma = pltpu.SemaphoreType.DMA
    return pl.pallas_call(
        best_kernel,
        out_shape=jax.ShapeDtypeStruct((1, ROWS), jnp.float32),
        in_specs=[
            pl.BlockSpec(memory_space=pl.ANY),
            pl.BlockSpec(memory_space=pl.ANY),
            pl.BlockSpec(memory_space=pltpu.SMEM),
        ],
        out_specs=pl.BlockSpec(memory_space=pltpu.VMEM),
        scratch_shapes=[
            pltpu.VMEM((8 * ROWS, D), jnp.bfloat16),
            pltpu.VMEM((HALF, D), jnp.bfloat16),
            pltpu.VMEM((HALF, D), jnp.bfloat16),
            pltpu.VMEM((8, 8 * ROWS), jnp.float32),
            pltpu.VMEM((8, 8 * ROWS), jnp.float32),
            pltpu.VMEM((7, 1, ROWS), jnp.float32),
            pltpu.VMEM((7, 1, ROWS), jnp.float32),
            dma((5,)),
            dma((1,)),
            dma((2, 4)), dma((2, 4)), dma((2, 2)), dma((2, 2)), dma((7,)), dma((7,)),
            dma((4,)), dma((4,)), dma((2, 4)), dma((2, 4)), dma((4,)), dma((4,)), dma((7,)), dma((7,)),
        ],
        compiler_params=pltpu.CompilerParams(
            collective_id=0, has_side_effects=True, vmem_limit_bytes=56 << 20
        ),
        cost_estimate=pl.CostEstimate(flops=2 * 8 * 512 * 4096 * 768, bytes_accessed=10 << 20, transcendentals=0),
    )(new_rows, index_rows, pattern).reshape(ROWS)


def per_device(new_rows, index_rows, pattern, kept_row, kept_owner, kept_local):
    cycle = lax.axis_size("blk")
    lanes = lax.axis_size("slab")
    best = best_of(new_rows, index_rows, pattern)
    new_unit = unit_rows(new_rows)
    picked = new_unit[kept_row]
    owner = kept_owner[:, 0]
    devices = cycle * lanes
    entries = kept_row.shape[0]
    local_tags = (kept_local[:, None] == jnp.arange(CL_DEV, dtype=jnp.int32)[None, :]).astype(
        jnp.bfloat16
    )
    capacity = (entries + devices - 1) // devices * 2
    position = jnp.arange(entries, dtype=jnp.int32)
    same_owner = owner[:, None] == owner[None, :]
    earlier = position[:, None] > position[None, :]
    rank = jnp.sum((same_owner & earlier).astype(jnp.int32), axis=1)
    target = owner * capacity + rank
    placing = (jnp.arange(devices * capacity, dtype=jnp.int32)[:, None] == target[None, :]).astype(
        jnp.bfloat16
    )
    payload = jnp.dot(placing, picked, preferred_element_type=jnp.float32).astype(jnp.bfloat16)
    tagging = jnp.dot(placing, local_tags, preferred_element_type=jnp.float32).astype(jnp.bfloat16)
    got_rows, got_tags = sent_together((payload, tagging), ("blk", "slab"), 0, 0, 1)
    sums = lax.dot_general(
        got_tags, got_rows, (((0,), (0,)), ((), ())), preferred_element_type=jnp.float32
    )
    counts = jnp.sum(got_tags.astype(jnp.float32), axis=0)
    return (best, sums, counts)


def solution(mesh):
    placed = (
        P(("blk", "slab"), None),
        P("blk", None),
        P(),
        P(("blk", "slab")),
        P(("blk", "slab"), None),
        P(("blk", "slab")),
    )
    return jax.shard_map(
        per_device,
        mesh=mesh,
        in_specs=placed,
        out_specs=(P(("blk", "slab")), P(("blk", "slab"), None), P(("blk", "slab"))),
        check_vma=False,
    )
```

```python
import jax
import jax.numpy as jnp
from jax import lax
from jax.experimental import pallas as pl
from jax.experimental.pallas import tpu as pltpu
from jax.sharding import PartitionSpec as P

CL_DEV = 16
EPS = 1e-06
MESH = pl.DeviceIdType.MESH
ROWS = 512
KEEP = 256
CH = 128
D = 768
HALF = 2048
UC = 96
UNIT = 4 * UC
COMMON = 512
WIDE = D + 128
PLANE = 256


def unit_rows(values):
    wide = values.astype(jnp.float32)
    scale = lax.rsqrt(jnp.sum(wide * wide, axis=-1, keepdims=True) + EPS)
    return (wide * scale).astype(jnp.bfloat16)


def ring4(v):
    return lax.rem(v + 4, 4)


def quad_at(k):
    return 2 * ROWS + ROWS * k


def places(dz, dc):
    side = 2 * CH * dc
    if dz == 0:
        return [ROWS * dc + CH * q for q in range(4)]
    if dz == 3:
        return [quad_at(q) + side for q in range(4)]
    if dz == 1:
        return [quad_at((q + 2) % 4) + side + CH for q in range(4)]
    return [quad_at(4 + q % 2) + side + CH * (q // 2) for q in range(4)]


CR_AT = (0, UC, 4 * UC, 5 * UC)
XM_AT = (2 * UC, 6 * UC, 8 * UC, 10 * UC)
XP_AT = (3 * UC, 7 * UC, 9 * UC, 11 * UC)
X2_AT = (12 * UC, 13 * UC, 14 * UC, 15 * UC)
AC_AT = (16 * UC, 16 * UC + CH)
AY_AT = (16 * UC + 2 * CH, 16 * UC + 3 * CH)


def window_kernel(
    new_hbm, index_hbm, pattern_hbm, row_hbm, owner_hbm, local_hbm, best_ref, sums_ref, counts_ref,
    nr, ir, oi, acc0, acc1, ret_out, ret_in, pattern, kept, codes, weights, partial, got,
    load_sem, z_s, z_r, z2_s, z2_r, sib_s, sib_r, cr_s, cr_r, ac_s, ac_r, ay_s, ay_r,
    x_s, x_r, x2_s, x2_r, ret_s, ret_r, code_s, code_r, sum_s, sum_r,
):
    b = lax.axis_index("blk")
    s = lax.axis_index("slab")
    z, h = lax.div(b, 2), lax.rem(b, 2)
    x, l, c = lax.div(s, 4), lax.rem(lax.div(s, 2), 2), lax.rem(s, 2)

    def blk_of(dz, dh=0):
        return ring4(z + dz) * 2 + (1 - h if dh else h)

    def slab_of(dx=0, dl=0, dc=0):
        return (ring4(x + dx) * 2 + (1 - l if dl else l)) * 2 + (1 - c if dc else c)

    zp, zm = (blk_of(1), s), (blk_of(-1), s)
    xp, xm = (b, slab_of(1)), (b, slab_of(-1))
    sib = (b, slab_of(0, 0, 1))
    cross = (blk_of(0, 1), slab_of(0, 1, 0))
    ylo = (b, slab_of(0, 1, 0))
    back = [(dz, dc) for dz in (0, 1, 2, 3) for dc in (0, 1) if (dz, dc) != (0, 0)]
    back_id = [(blk_of(dz), slab_of(0, 0, dc)) for dz, dc in back]
    plane = [(dh, dx, dl) for dx in (0, 1, 3, 2) for dh in (0, 1) for dl in (0, 1) if (dh, dx, dl) != (0, 0, 0)]
    plane_id = [(blk_of(0, dh), slab_of(dx, dl)) for dh, dx, dl in plane]
    partners = back_id + plane_id

    barrier = pltpu.get_barrier_semaphore()
    for p in partners:
        pl.semaphore_signal(barrier, inc=1, device_id=p, device_id_type=MESH)

    def rows(ref, at, n=CH):
        return ref.at[pl.ds(at, n)]

    loads = [pltpu.make_async_copy(new_hbm, rows(nr, 0, ROWS), load_sem.at[0])]
    half_to = pl.multiple_of((1 - l) * (COMMON // 2), 128)
    half_here = pl.multiple_of(l * (COMMON // 2), 128)
    index_parts = [(pl.multiple_of(COMMON + x * UNIT, 128), UNIT), (half_to, COMMON // 2), (half_here, COMMON // 2)]
    index_parts += [(pl.multiple_of(COMMON + ring4(x + j) * UNIT, 128), UNIT) for j in (1, 2, 3)]
    for j, (at, n) in enumerate(index_parts):
        loads.append(
            pltpu.make_async_copy(
                index_hbm.at[pl.ds(pl.multiple_of(c * HALF + at, 128), n)], rows(ir, at, n), load_sem.at[1 + j]
            )
        )
    small = [
        pltpu.make_async_copy(ref, kept.at[j], load_sem.at[7 + j])
        for j, ref in enumerate((row_hbm, owner_hbm, local_hbm))
    ]
    small.append(pltpu.make_async_copy(pattern_hbm, pattern, load_sem.at[10]))
    for cp in loads + small:
        cp.start()

    def remote(src, dst, ss, rs, dev):
        return pltpu.make_async_remote_copy(
            src_ref=src, dst_ref=dst, send_sem=ss, recv_sem=rs, device_id=dev, device_id_type=MESH
        )

    own_p = [remote(rows(nr, CH * k), rows(nr, quad_at(k)), z_s.at[0, k], z_r.at[0, k], zp) for k in range(4)]
    own_m = [
        remote(rows(nr, CH * ((k + 2) % 4)), rows(nr, quad_at(k) + CH), z_s.at[1, k], z_r.at[1, k], zm)
        for k in range(4)
    ]
    fwd_p = [remote(rows(nr, quad_at(k)), rows(nr, quad_at(4 + k)), z2_s.at[0, k], z2_r.at[0, k], zp) for k in range(2)]
    fwd_m = [
        remote(rows(nr, quad_at(k) + CH), rows(nr, quad_at(4 + k) + CH), z2_s.at[1, k], z2_r.at[1, k], zm)
        for k in range(2)
    ]
    to_sib = [remote(rows(nr, 0, ROWS), rows(nr, ROWS, ROWS), sib_s.at[6], sib_r.at[6], sib)]
    pair_sib = [
        remote(rows(nr, quad_at(k), 2 * CH), rows(nr, quad_at(k) + 2 * CH, 2 * CH), sib_s.at[k], sib_r.at[k], sib)
        for k in range(6)
    ]
    unit_at = [pl.multiple_of(COMMON + x * UNIT + UC * k, 32) for k in range(4)]
    cr = [remote(rows(ir, unit_at[k], UC), rows(oi, CR_AT[k], UC), cr_s.at[k], cr_r.at[k], cross) for k in range(4)]
    common_at = [pl.multiple_of(half_to + CH * k, CH) for k in range(2)]
    ac = [remote(rows(ir, common_at[k]), rows(oi, AC_AT[k]), ac_s.at[k], ac_r.at[k], cross) for k in range(2)]
    ay = [remote(rows(oi, AC_AT[k]), rows(oi, AY_AT[k]), ay_s.at[k], ay_r.at[k], ylo) for k in range(2)]
    x_p = [remote(rows(oi, CR_AT[k], UC), rows(oi, XM_AT[k], UC), x_s.at[0, k], x_r.at[0, k], xp) for k in range(4)]
    x_m = [remote(rows(oi, CR_AT[k], UC), rows(oi, XP_AT[k], UC), x_s.at[1, k], x_r.at[1, k], xm) for k in range(4)]
    x_f = [
        remote(rows(oi, (XP_AT if k % 2 else XM_AT)[k], UC), rows(oi, X2_AT[k], UC), x2_s.at[k], x2_r.at[k], xm if k % 2 else xp)
        for k in range(4)
    ]
    code = [remote(codes.at[0], codes.at[1 + i], code_s.at[i], code_r.at[i], dev) for i, dev in enumerate(back_id)]

    def place_of(dh, dx, dl):
        return (1 - h if dh else h) * 8 + ring4(x + dx) * 2 + (1 - l if dl else l)

    def cluster_rows(dh, dx, dl):
        return pl.ds(pl.multiple_of(place_of(dh, dx, dl) * CL_DEV, CL_DEV), CL_DEV)

    sums = [
        remote(partial.at[cluster_rows(*plane[j])], got.at[j], sum_s.at[j], sum_r.at[j], plane_id[j])
        for j in range(len(plane))
    ]

    acc0[...] = jnp.full(acc0.shape, -3.0, jnp.float32)
    acc1[...] = jnp.full(acc1.shape, -3.0, jnp.float32)

    def normalize(ref, at, n=CH):
        ref[pl.ds(at, n), :] = unit_rows(ref[pl.ds(at, n), :])

    loads[0].wait()
    normalize(nr, 0)
    normalize(nr, 2 * CH)
    normalize(nr, CH)
    normalize(nr, 3 * CH)
    loads[1].wait()
    for k in range(4):
        normalize(ir, unit_at[k], UC)
    for cp in small:
        cp.wait()
    codes[0] = (kept[1] * CL_DEV + kept[2]) * ROWS + kept[0]
    pl.semaphore_wait(barrier, len(partners))
    for k in range(4):
        own_p[k].start()
        own_m[k].start()
        cr[k].start()
    to_sib[0].start()
    for cp in code:
        cp.start()
    loads[2].wait()
    for k in range(2):
        normalize(ir, common_at[k])
        ac[k].start()
    for j in range(2, 6):
        loads[1 + j].wait()
        at, n = index_parts[j]
        for k in range(n // CH):
            normalize(ir, pl.multiple_of(at + CH * k, CH))

    def scores(acc, idx, i_at, i_n, n_at, n_n):
        prod = lax.dot_general(
            idx[pl.ds(i_at, i_n), :], nr[pl.ds(n_at, n_n), :],
            (((1,), (1,)), ((), ())), preferred_element_type=jnp.float32,
        )
        top = jnp.max(prod.reshape(i_n // 8, 8, n_n), axis=0)
        acc[:, pl.ds(n_at, n_n)] = jnp.maximum(acc[:, pl.ds(n_at, n_n)], top)

    def own_range(n_at):
        scores(acc0, ir, 0, HALF, n_at, ROWS)

    def other_range(i_at, i_end, n_at, n_end):
        scores(acc1, oi, i_at, i_end - i_at, n_at, n_end - n_at)

    def z_in(k):
        if k < 4:
            own_p[k].wait_recv()
            if k < 2:
                fwd_p[k].start()
            own_m[k].wait_recv()
            if k < 2:
                fwd_m[k].start()
        else:
            fwd_p[k - 4].wait_recv()
            fwd_m[k - 4].wait_recv()
        pair_sib[k].start()

    def cross_in(k):
        cr[k].wait_recv()
        x_p[k].start()
        x_m[k].start()

    def common_in(k):
        ac[k].wait_recv()
        ay[k].start()

    def x_in(k):
        x_p[k].wait_recv()
        if k % 2 == 0:
            x_f[k].start()
        x_m[k].wait_recv()
        if k % 2 == 1:
            x_f[k].start()

    def quad(k):
        pair_sib[k].wait_recv()
        own_range(quad_at(k))

    def weigh(slot, dz, dc):
        both = codes[slot]
        row = lax.rem(both, ROWS)
        local = lax.rem(lax.div(both, ROWS), CL_DEV)
        owner = lax.div(both, ROWS * CL_DEV)
        o_blk, o_slab = lax.div(owner, 16), lax.rem(owner, 16)
        mine = (lax.div(o_blk, 2) == z) & (lax.rem(o_slab, 2) == c)
        cluster = (lax.rem(o_blk, 2) * 8 + lax.div(o_slab, 2)) * CL_DEV + local
        cluster = jnp.where(mine, cluster, -1)

        def hot(count, which):
            at = lax.broadcasted_iota(jnp.int32, (count, KEEP), 0)
            return jnp.where(at == which, 1.0, 0.0).astype(jnp.bfloat16)

        named = lax.dot_general(
            hot(PLANE, cluster), hot(ROWS, row), (((1,), (1,)), ((), ())), preferred_element_type=jnp.float32
        )
        for q, at in enumerate(places(dz, dc)):
            weights[:, pl.ds(at, CH)] = named[:, CH * q : CH * (q + 1)].astype(jnp.bfloat16)
        return jnp.sum(named, axis=1, keepdims=True)

    def add_rows(n_at, n_end, first):
        part = jnp.dot(
            weights[:, pl.ds(n_at, n_end - n_at)], nr[pl.ds(n_at, n_end - n_at), :], preferred_element_type=jnp.float32
        )
        partial[:, pl.ds(0, D)] = part if first else partial[:, pl.ds(0, D)] + part

    own_range(0)
    to_sib[0].wait_recv()
    own_range(ROWS)
    cross_in(0)
    z_in(0)
    count = weigh(0, 0, 0)
    for i, (dz, dc) in enumerate(back):
        code[i].wait_recv()
        count = count + weigh(1 + i, (4 - dz) % 4, dc)
        if i == 3:
            cross_in(1)
    partial[:, pl.ds(D, 128)] = jnp.broadcast_to(count, (PLANE, 128))
    quad(0)
    x_in(0)
    z_in(1)
    cross_in(2)
    quad(1)
    x_in(1)
    cross_in(3)
    other_range(0, 4 * UC, 0, 2048)
    z_in(2)
    quad(2)
    x_in(2)
    other_range(4 * UC, 8 * UC, 0, 2048)
    z_in(3)
    common_in(0)
    quad(3)
    x_in(3)
    other_range(0, 8 * UC, 2048, 3072)
    common_in(1)
    other_range(8 * UC, 12 * UC, 0, 3072)
    add_rows(0, 3072, True)
    z_in(4)
    quad(4)
    for k in range(4):
        x_f[k].wait_recv()
    other_range(12 * UC, 16 * UC + 2 * CH, 0, 3072)
    z_in(5)
    pair_sib[5].wait_recv()
    add_rows(3072, 4096, False)
    for cp in sums:
        cp.start()
    own_range(quad_at(5))
    other_range(0, 16 * UC + 2 * CH, 3072, 4096)
    for cp in ay:
        cp.wait_recv()
    other_range(16 * UC + 2 * CH, HALF, 0, 4096)

    def block_best(dz, dc):
        row = blk_of(dz) * 16 + slab_of(0, 0, dc)
        live0 = jnp.full((1, ROWS), pattern[b, row], jnp.int32) > 0
        live1 = jnp.full((1, ROWS), pattern[blk_of(0, 1), row], jnp.int32) > 0

        def top(acc):
            parts = [jnp.max(acc[:, pl.ds(w, CH)], axis=0, keepdims=True) for w in places(dz, dc)]
            return jnp.concatenate(parts, axis=1)

        return jnp.maximum(jnp.where(live0, top(acc0), -2.0), jnp.where(live1, top(acc1), -2.0))

    rets = []
    for i, (dz, dc) in enumerate(back):
        ret_out[i] = block_best(dz, dc)
        cp = remote(ret_out.at[i], ret_in.at[i], ret_s.at[i], ret_r.at[i], back_id[i])
        cp.start()
        rets.append(cp)
    best = block_best(0, 0)
    total = partial[cluster_rows(0, 0, 0), :]
    for j, cp in enumerate(sums):
        cp.wait_recv()
        total = total + got[j]
    sums_ref[...] = total[:, :D]
    counts_ref[...] = total[:, D:]
    for i, cp in enumerate(rets):
        cp.wait_recv()
        best = jnp.maximum(best, ret_in[i])
    best_ref[...] = best
    for cp in own_p + own_m + fwd_p + fwd_m + to_sib + pair_sib + cr + ac + ay + x_p + x_m + x_f + code + sums + rets:
        cp.wait_send()


def per_device(new_rows, index_rows, pattern, kept_row, kept_owner, kept_local):
    dma = pltpu.SemaphoreType.DMA
    f32, bf16, i32 = jnp.float32, jnp.bfloat16, jnp.int32
    best, sums, counts = pl.pallas_call(
        window_kernel,
        out_shape=(
            jax.ShapeDtypeStruct((1, ROWS), f32),
            jax.ShapeDtypeStruct((CL_DEV, D), f32),
            jax.ShapeDtypeStruct((CL_DEV, 128), f32),
        ),
        in_specs=[pl.BlockSpec(memory_space=pl.ANY)] * 6,
        out_specs=[pl.BlockSpec(memory_space=pltpu.VMEM)] * 3,
        scratch_shapes=[
            pltpu.VMEM((8 * ROWS, D), bf16),
            pltpu.VMEM((HALF, D), bf16),
            pltpu.VMEM((HALF, D), bf16),
            pltpu.VMEM((8, 8 * ROWS), f32),
            pltpu.VMEM((8, 8 * ROWS), f32),
            pltpu.VMEM((7, 1, ROWS), f32),
            pltpu.VMEM((7, 1, ROWS), f32),
            pltpu.SMEM((8, 128), i32),
            pltpu.VMEM((3, 1, KEEP), i32),
            pltpu.VMEM((8, 1, KEEP), i32),
            pltpu.VMEM((PLANE, 8 * ROWS), bf16),
            pltpu.VMEM((PLANE, WIDE), f32),
            pltpu.VMEM((15, CL_DEV, WIDE), f32),
            dma((11,)),
            dma((2, 4)), dma((2, 4)), dma((2, 2)), dma((2, 2)), dma((7,)), dma((7,)), dma((4,)), dma((4,)),
            dma((2,)), dma((2,)), dma((2,)), dma((2,)),
            dma((2, 4)), dma((2, 4)), dma((4,)), dma((4,)), dma((7,)), dma((7,)), dma((7,)), dma((7,)),
            dma((15,)), dma((15,)),
        ],
        compiler_params=pltpu.CompilerParams(
            collective_id=0, has_side_effects=True, vmem_limit_bytes=56 << 20
        ),
        cost_estimate=pl.CostEstimate(flops=2 * 8 * 512 * 4096 * 768, bytes_accessed=10 << 20, transcendentals=0),
    )(
        new_rows,
        index_rows,
        pattern.T,
        kept_row.reshape(1, KEEP),
        kept_owner.reshape(1, KEEP),
        kept_local.reshape(1, KEEP),
    )
    return (best.reshape(ROWS), sums, counts[:, 0])


def solution(mesh):
    placed = (
        P(("blk", "slab"), None),
        P("blk", None),
        P(),
        P(("blk", "slab")),
        P(("blk", "slab"), None),
        P(("blk", "slab")),
    )
    return jax.shard_map(
        per_device,
        mesh=mesh,
        in_specs=placed,
        out_specs=(P(("blk", "slab")), P(("blk", "slab"), None), P(("blk", "slab"))),
        check_vma=False,
    )
```

```python
import jax
import jax.numpy as jnp
from jax import lax
from jax.experimental import pallas as pl
from jax.experimental.pallas import tpu as pltpu
from jax.sharding import PartitionSpec as P

CL_DEV = 16
EPS = 1e-06
MESH = pl.DeviceIdType.MESH
ROWS = 512
KEEP = 256
CH = 128
D = 768
HALF = 2048
UC = 96
UNIT = 4 * UC
COMMON = 512
WIDE = D + 128
PLANE = 256


def unit_rows(values):
    wide = values.astype(jnp.float32)
    scale = lax.rsqrt(jnp.sum(wide * wide, axis=-1, keepdims=True) + EPS)
    return (wide * scale).astype(jnp.bfloat16)


def ring4(v):
    return lax.rem(v + 4, 4)


def quad_at(k):
    return 2 * ROWS + ROWS * k


def places(dz, dc):
    side = 2 * CH * dc
    if dz == 0:
        return [ROWS * dc + CH * q for q in range(4)]
    if dz == 3:
        return [quad_at(q) + side for q in range(4)]
    if dz == 1:
        return [quad_at((q + 2) % 4) + side + CH for q in range(4)]
    return [quad_at(4 + q % 2) + side + CH * (q // 2) for q in range(4)]


CR_AT = (0, UC, 2 * UC, 3 * UC)
XM_AT = (384, 576, 1088, 768)
XP_AT = (480, 672, 1184, 864)
AC_AT = (960, 1280)
X2_AT = (1408, 1504, 1600, 1696)
AY_AT = (1792, 1920)


def window_kernel(
    new_hbm, index_hbm, pattern_hbm, row_hbm, owner_hbm, local_hbm, best_ref, sums_ref,
    nr, ir, oi, acc0, acc1, ret_out, ret_in, pattern, kept, codes, weights, partial, got,
    load_sem, z_s, z_r, z2_s, z2_r, sib_s, sib_r, cr_s, cr_r, yu_s, yu_r, ac_s, ac_r, ay_s, ay_r,
    x_s, x_r, x2_s, x2_r, ret_s, ret_r, code_s, code_r, sum_s, sum_r,
):
    b = lax.axis_index("blk")
    s = lax.axis_index("slab")
    z, h = lax.div(b, 2), lax.rem(b, 2)
    x, l, c = lax.div(s, 4), lax.rem(lax.div(s, 2), 2), lax.rem(s, 2)

    def blk_of(dz, dh=0):
        return ring4(z + dz) * 2 + (1 - h if dh else h)

    def slab_of(dx=0, dl=0, dc=0):
        return (ring4(x + dx) * 2 + (1 - l if dl else l)) * 2 + (1 - c if dc else c)

    zp, zm = (blk_of(1), s), (blk_of(-1), s)
    xp, xm = (b, slab_of(1)), (b, slab_of(-1))
    sib = (b, slab_of(0, 0, 1))
    cross = (blk_of(0, 1), slab_of(0, 1, 0))
    ylo = (b, slab_of(0, 1, 0))
    back = [(2, 0), (2, 1), (1, 0), (3, 0), (1, 1), (3, 1), (0, 1)]
    back_id = [(blk_of(dz), slab_of(0, 0, dc)) for dz, dc in back]
    plane = [(dh, dx, dl) for dx in (0, 1, 3, 2) for dh in (0, 1) for dl in (0, 1) if (dh, dx, dl) != (0, 0, 0)]
    plane_id = [(blk_of(0, dh), slab_of(dx, dl)) for dh, dx, dl in plane]
    partners = back_id + plane_id

    barrier = pltpu.get_barrier_semaphore()
    for p in partners:
        pl.semaphore_signal(barrier, inc=1, device_id=p, device_id_type=MESH)

    def rows(ref, at, n=CH):
        return ref.at[pl.ds(at, n)]

    loads = [pltpu.make_async_copy(new_hbm, rows(nr, 0, ROWS), load_sem.at[0])]
    half_to = pl.multiple_of((1 - l) * (COMMON // 2), 128)
    half_here = pl.multiple_of(l * (COMMON // 2), 128)
    index_parts = [(pl.multiple_of(COMMON + x * UNIT, 128), UNIT), (half_to, COMMON // 2), (half_here, COMMON // 2)]
    index_parts += [(pl.multiple_of(COMMON + ring4(x + j) * UNIT, 128), UNIT) for j in (1, 2, 3)]
    for j, (at, n) in enumerate(index_parts):
        loads.append(
            pltpu.make_async_copy(
                index_hbm.at[pl.ds(pl.multiple_of(c * HALF + at, 128), n)], rows(ir, at, n), load_sem.at[1 + j]
            )
        )
    small = [
        pltpu.make_async_copy(ref, kept.at[j], load_sem.at[7 + j])
        for j, ref in enumerate((row_hbm, owner_hbm, local_hbm))
    ]
    small.append(pltpu.make_async_copy(pattern_hbm, pattern, load_sem.at[10]))
    for cp in loads + small:
        cp.start()

    def remote(src, dst, ss, rs, dev):
        return pltpu.make_async_remote_copy(
            src_ref=src, dst_ref=dst, send_sem=ss, recv_sem=rs, device_id=dev, device_id_type=MESH
        )

    own_p = [remote(rows(nr, CH * k), rows(nr, quad_at(k)), z_s.at[0, k], z_r.at[0, k], zp) for k in range(4)]
    own_m = [
        remote(rows(nr, CH * ((k + 2) % 4)), rows(nr, quad_at(k) + CH), z_s.at[1, k], z_r.at[1, k], zm)
        for k in range(4)
    ]
    fwd_p = [remote(rows(nr, quad_at(k)), rows(nr, quad_at(4 + k)), z2_s.at[0, k], z2_r.at[0, k], zp) for k in range(2)]
    fwd_m = [
        remote(rows(nr, quad_at(k) + CH), rows(nr, quad_at(4 + k) + CH), z2_s.at[1, k], z2_r.at[1, k], zm)
        for k in range(2)
    ]
    to_sib = [remote(rows(nr, 0, ROWS), rows(nr, ROWS, ROWS), sib_s.at[6], sib_r.at[6], sib)]
    pair_sib = [
        remote(rows(nr, quad_at(k), 2 * CH), rows(nr, quad_at(k) + 2 * CH, 2 * CH), sib_s.at[k], sib_r.at[k], sib)
        for k in range(6)
    ]
    unit_at = [pl.multiple_of(COMMON + x * UNIT + UC * k, 32) for k in (3 * (1 - l), 1, 2, 3 * l)]
    cr = [remote(rows(ir, unit_at[k], UC), rows(oi, CR_AT[k], UC), cr_s.at[k], cr_r.at[k], cross) for k in range(3)]
    yu = [remote(rows(oi, CR_AT[0], UC), rows(oi, CR_AT[3], UC), yu_s.at[0], yu_r.at[0], ylo)]
    common_at = [pl.multiple_of(half_to + CH * k, CH) for k in range(2)]
    ac = [remote(rows(ir, common_at[k]), rows(oi, AC_AT[k]), ac_s.at[k], ac_r.at[k], cross) for k in range(2)]
    ay = [remote(rows(oi, AC_AT[k]), rows(oi, AY_AT[k]), ay_s.at[k], ay_r.at[k], ylo) for k in range(2)]
    x_p = [remote(rows(oi, CR_AT[k], UC), rows(oi, XM_AT[k], UC), x_s.at[0, k], x_r.at[0, k], xp) for k in range(4)]
    x_m = [remote(rows(oi, CR_AT[k], UC), rows(oi, XP_AT[k], UC), x_s.at[1, k], x_r.at[1, k], xm) for k in range(4)]
    x_f = [
        remote(rows(oi, (XP_AT if k % 2 else XM_AT)[k], UC), rows(oi, X2_AT[k], UC), x2_s.at[k], x2_r.at[k], xm if k % 2 else xp)
        for k in range(4)
    ]
    code = [remote(codes.at[0], codes.at[1 + i], code_s.at[i], code_r.at[i], dev) for i, dev in enumerate(back_id)]

    def place_of(dh, dx, dl):
        return (1 - h if dh else h) * 8 + ring4(x + dx) * 2 + (1 - l if dl else l)

    def cluster_rows(dh, dx, dl):
        return pl.ds(pl.multiple_of(place_of(dh, dx, dl) * CL_DEV, CL_DEV), CL_DEV)

    sums = [
        remote(partial.at[cluster_rows(*plane[j])], got.at[j], sum_s.at[j], sum_r.at[j], plane_id[j])
        for j in range(len(plane))
    ]

    acc0[...] = jnp.full(acc0.shape, -3.0, jnp.float32)
    acc1[...] = jnp.full(acc1.shape, -3.0, jnp.float32)

    def normalize(ref, at, n=CH):
        ref[pl.ds(at, n), :] = unit_rows(ref[pl.ds(at, n), :])

    loads[0].wait()
    normalize(nr, 0)
    normalize(nr, 2 * CH)
    normalize(nr, CH)
    normalize(nr, 3 * CH)
    loads[1].wait()
    for k in range(4):
        normalize(ir, unit_at[k], UC)
    for cp in small:
        cp.wait()
    codes[0] = (kept[1] * CL_DEV + kept[2]) * ROWS + kept[0]
    pl.semaphore_wait(barrier, len(partners))
    for cp in code:
        cp.start()
    for k in range(4):
        own_p[k].start()
        own_m[k].start()
    for cp in cr:
        cp.start()
    to_sib[0].start()
    loads[2].wait()
    for k in range(2):
        normalize(ir, common_at[k])
        ac[k].start()
    for j in range(2, 6):
        loads[1 + j].wait()
        at, n = index_parts[j]
        for k in range(n // CH):
            normalize(ir, pl.multiple_of(at + CH * k, CH))

    def scores(acc, idx, i_at, i_n, n_at, n_n):
        prod = lax.dot_general(
            idx[pl.ds(i_at, i_n), :], nr[pl.ds(n_at, n_n), :],
            (((1,), (1,)), ((), ())), preferred_element_type=jnp.float32,
        )
        top = jnp.max(prod.reshape(i_n // 8, 8, n_n), axis=0)
        acc[:, pl.ds(n_at, n_n)] = jnp.maximum(acc[:, pl.ds(n_at, n_n)], top)

    def own_range(n_at):
        scores(acc0, ir, 0, HALF, n_at, ROWS)

    def other_range(i_at, i_end, n_at, n_end):
        scores(acc1, oi, i_at, i_end - i_at, n_at, n_end - n_at)

    def z_in(k):
        if k < 4:
            own_p[k].wait_recv()
            if k < 2:
                fwd_p[k].start()
            own_m[k].wait_recv()
            if k < 2:
                fwd_m[k].start()
        else:
            fwd_p[k - 4].wait_recv()
            fwd_m[k - 4].wait_recv()
        pair_sib[k].start()

    def cross_in(k):
        (cr + yu)[k].wait_recv()
        if k == 0:
            yu[0].start()
        x_p[k].start()
        x_m[k].start()

    def common_in(k):
        ac[k].wait_recv()
        ay[k].start()

    def x_in(k):
        x_p[k].wait_recv()
        if k % 2 == 0:
            x_f[k].start()
        x_m[k].wait_recv()
        if k % 2 == 1:
            x_f[k].start()

    def quad(k):
        pair_sib[k].wait_recv()
        own_range(quad_at(k))

    def weigh(slot, dz, dc):
        both = codes[slot]
        row = lax.rem(both, ROWS)
        local = lax.rem(lax.div(both, ROWS), CL_DEV)
        owner = lax.div(both, ROWS * CL_DEV)
        o_blk, o_slab = lax.div(owner, 16), lax.rem(owner, 16)
        mine = (lax.div(o_blk, 2) == z) & (lax.rem(o_slab, 2) == c)
        cluster = (lax.rem(o_blk, 2) * 8 + lax.div(o_slab, 2)) * CL_DEV + local
        cluster = jnp.where(mine, cluster, -1)

        def hot(count, which):
            at = lax.broadcasted_iota(jnp.int32, (count, KEEP), 0)
            return jnp.where(at == which, 1.0, 0.0).astype(jnp.bfloat16)

        named = lax.dot_general(
            hot(PLANE, cluster), hot(ROWS, row), (((1,), (1,)), ((), ())), preferred_element_type=jnp.float32
        )
        for q, at in enumerate(places(dz, dc)):
            weights[:, pl.ds(at, CH)] = named[:, CH * q : CH * (q + 1)].astype(jnp.bfloat16)
        return jnp.sum(named, axis=1, keepdims=True)

    def add_rows(n_at, n_end, first):
        part = jnp.dot(
            weights[:, pl.ds(n_at, n_end - n_at)], nr[pl.ds(n_at, n_end - n_at), :], preferred_element_type=jnp.float32
        )
        partial[:, pl.ds(0, D)] = part if first else partial[:, pl.ds(0, D)] + part

    own_range(0)
    count = weigh(0, 0, 0)
    to_sib[0].wait_recv()
    own_range(ROWS)
    cross_in(0)
    for i, (dz, dc) in enumerate(back):
        code[i].wait_recv()
        count = count + weigh(1 + i, (4 - dz) % 4, dc)
        if i == 3:
            z_in(0)
    partial[:, pl.ds(D, 128)] = jnp.broadcast_to(count, (PLANE, 128))
    cross_in(1)
    quad(0)
    cross_in(3)
    x_in(0)
    z_in(1)
    cross_in(2)
    quad(1)
    x_in(1)
    other_range(0, 768, 512, 2048)
    z_in(2)
    quad(2)
    other_range(0, 768, 2048, 2560)
    common_in(0)
    x_in(3)
    z_in(3)
    other_range(768, 1088, 512, 2560)
    quad(3)
    x_in(2)
    common_in(1)
    other_range(0, 1088, 2560, 3072)
    z_in(4)
    other_range(1088, 1408, 512, 3072)
    quad(4)
    add_rows(0, 3072, True)
    other_range(0, 1408, 3072, 3584)
    z_in(5)
    pair_sib[5].wait_recv()
    add_rows(3072, 4096, False)
    for cp in sums:
        cp.start()
    own_range(quad_at(5))
    for k in range(4):
        x_f[k].wait_recv()
    for cp in ay:
        cp.wait_recv()
    other_range(1408, HALF, 512, 3584)
    other_range(0, HALF, 3584, 4096)

    def block_best(dz, dc):
        row = blk_of(dz) * 16 + slab_of(0, 0, dc)
        live0 = jnp.full((8, CH), pattern[b, row], jnp.int32) > 0
        live1 = jnp.full((8, CH), pattern[blk_of(0, 1), row], jnp.int32) > 0
        parts = []
        for w in places(dz, dc):
            here = jnp.where(live0, acc0[:, pl.ds(w, CH)], -2.0)
            there = jnp.where(live1, acc1[:, pl.ds(w, CH)], -2.0)
            parts.append(jnp.max(jnp.maximum(here, there), axis=0, keepdims=True))
        return jnp.concatenate(parts, axis=1)

    rets = []
    for i, (dz, dc) in enumerate(back):
        ret_out[i] = block_best(dz, dc)
        cp = remote(ret_out.at[i], ret_in.at[i], ret_s.at[i], ret_r.at[i], back_id[i])
        cp.start()
        rets.append(cp)
    other_range(0, HALF, 0, 512)
    best = block_best(0, 0)
    total = partial[cluster_rows(0, 0, 0), :]
    for j, cp in enumerate(sums):
        cp.wait_recv()
        total = total + got[j]
    sums_ref[...] = total
    for i, cp in enumerate(rets):
        cp.wait_recv()
        best = jnp.maximum(best, ret_in[i])
    best_ref[...] = best
    for cp in own_p + own_m + fwd_p + fwd_m + to_sib + pair_sib + cr + yu + ac + ay + x_p + x_m + x_f + code + sums + rets:
        cp.wait_send()


def parted(best_in, sums_in, best_ref, sums_ref, counts_ref):
    best_ref[...] = best_in[...]
    sums_ref[...] = sums_in[:, :D]
    counts = sums_in[:, D:]
    at = [lax.broadcasted_iota(jnp.int32, counts.shape, axis) for axis in (0, 1)]
    counts_ref[...] = jnp.sum(jnp.where(at[0] == at[1], counts, 0.0), axis=0, keepdims=True)[:, :CL_DEV]


def per_device(new_rows, index_rows, pattern, kept_row, kept_owner, kept_local):
    dma = pltpu.SemaphoreType.DMA
    f32, bf16, i32 = jnp.float32, jnp.bfloat16, jnp.int32
    best, sums = pl.pallas_call(
        window_kernel,
        out_shape=(
            jax.ShapeDtypeStruct((1, ROWS), f32),
            jax.ShapeDtypeStruct((CL_DEV, WIDE), f32),
        ),
        in_specs=[pl.BlockSpec(memory_space=pl.ANY)] * 6,
        out_specs=[pl.BlockSpec(memory_space=pltpu.VMEM)] * 2,
        scratch_shapes=[
            pltpu.VMEM((8 * ROWS, D), bf16),
            pltpu.VMEM((HALF, D), bf16),
            pltpu.VMEM((HALF, D), bf16),
            pltpu.VMEM((8, 8 * ROWS), f32),
            pltpu.VMEM((8, 8 * ROWS), f32),
            pltpu.VMEM((7, 1, ROWS), f32),
            pltpu.VMEM((7, 1, ROWS), f32),
            pltpu.SMEM((8, 128), i32),
            pltpu.VMEM((3, 1, KEEP), i32),
            pltpu.VMEM((8, 1, KEEP), i32),
            pltpu.VMEM((PLANE, 8 * ROWS), bf16),
            pltpu.VMEM((PLANE, WIDE), f32),
            pltpu.VMEM((15, CL_DEV, WIDE), f32),
            dma((11,)),
            dma((2, 4)), dma((2, 4)), dma((2, 2)), dma((2, 2)), dma((7,)), dma((7,)), dma((4,)), dma((4,)),
            dma((1,)), dma((1,)), dma((2,)), dma((2,)), dma((2,)), dma((2,)),
            dma((2, 4)), dma((2, 4)), dma((4,)), dma((4,)), dma((7,)), dma((7,)), dma((7,)), dma((7,)),
            dma((15,)), dma((15,)),
        ],
        compiler_params=pltpu.CompilerParams(
            collective_id=0, has_side_effects=True, vmem_limit_bytes=56 << 20
        ),
        cost_estimate=pl.CostEstimate(flops=2 * 8 * 512 * 4096 * 768, bytes_accessed=10 << 20, transcendentals=0),
    )(
        new_rows,
        index_rows,
        pattern.T,
        kept_row.reshape(1, KEEP),
        kept_owner.reshape(1, KEEP),
        kept_local.reshape(1, KEEP),
    )
    best, sums, counts = pl.pallas_call(
        parted,
        out_shape=(
            jax.ShapeDtypeStruct((1, ROWS), f32),
            jax.ShapeDtypeStruct((CL_DEV, D), f32),
            jax.ShapeDtypeStruct((1, CL_DEV), f32),
        ),
        in_specs=[pl.BlockSpec(memory_space=pltpu.VMEM)] * 2,
        out_specs=[pl.BlockSpec(memory_space=pltpu.VMEM)] * 3,
    )(best, sums)
    return (best.reshape(ROWS), sums, counts.reshape(CL_DEV))


def solution(mesh):
    placed = (
        P(("blk", "slab"), None),
        P("blk", None),
        P(),
        P(("blk", "slab")),
        P(("blk", "slab"), None),
        P(("blk", "slab")),
    )
    return jax.shard_map(
        per_device,
        mesh=mesh,
        in_specs=placed,
        out_specs=(P(("blk", "slab")), P(("blk", "slab"), None), P(("blk", "slab"))),
        check_vma=False,
    )
```

```python
import jax
import jax.numpy as jnp
from jax import lax
from jax.experimental import pallas as pl
from jax.experimental.pallas import tpu as pltpu
from jax.sharding import PartitionSpec as P

CL_DEV = 16
EPS = 1e-06
MESH = pl.DeviceIdType.MESH
ROWS = 512
KEEP = 256
CH = 128
D = 768
HALF = 2048
UC = 80
UNIT = 4 * UC
COMMON = 768
WIDE = D + 128
KCAP = 4
LATE = 3072
PLANE = 256


def unit_rows(values):
    wide = values.astype(jnp.float32)
    scale = lax.rsqrt(jnp.sum(wide * wide, axis=-1, keepdims=True) + EPS)
    return (wide * scale).astype(jnp.bfloat16)


def ring4(v):
    return lax.rem(v + 4, 4)


def quad_at(k):
    return 2 * ROWS + ROWS * k


def places(dz, dc):
    side = 2 * CH * dc
    if dz == 0:
        return [ROWS * dc + CH * q for q in range(4)]
    if dz == 3:
        return [quad_at(q) + side for q in range(4)]
    if dz == 1:
        return [quad_at((q + 2) % 4) + side + CH for q in range(4)]
    return [quad_at(4 + q % 2) + side + CH * (q // 2) for q in range(4)]


CR_AT = (0, UC, 2 * UC, 3 * UC)
XM_AT = (320, 480, 928, 640)
XP_AT = (400, 560, 1008, 720)
AC_AT = (800, 1088, 1536)
X2_AT = (1216, 1296, 1376, 1456)
AY_AT = (1664, 1792, 1920)


def window_kernel(
    new_hbm, index_hbm, pattern_hbm, row_hbm, owner_hbm, local_hbm, best_ref, sums_ref, counts_ref,
    nr, ir, oi, acc0, acc1, ret_out, ret_in, pattern, kept, codes, weights, partial, got,
    late_weights, late, late_got, tags, tally,
    load_sem, z_s, z_r, z2_s, z2_r, sib_s, sib_r, cr_s, cr_r, yu_s, yu_r, ac_s, ac_r, ay_s, ay_r,
    x_s, x_r, x2_s, x2_r, ret_s, ret_r, code_s, code_r, sum_s, sum_r, late_s, late_r,
):
    b = lax.axis_index("blk")
    s = lax.axis_index("slab")
    z, h = lax.div(b, 2), lax.rem(b, 2)
    x, l, c = lax.div(s, 4), lax.rem(lax.div(s, 2), 2), lax.rem(s, 2)

    def blk_of(dz, dh=0):
        return ring4(z + dz) * 2 + (1 - h if dh else h)

    def slab_of(dx=0, dl=0, dc=0):
        return (ring4(x + dx) * 2 + (1 - l if dl else l)) * 2 + (1 - c if dc else c)

    zp, zm = (blk_of(1), s), (blk_of(-1), s)
    xp, xm = (b, slab_of(1)), (b, slab_of(-1))
    sib = (b, slab_of(0, 0, 1))
    cross = (blk_of(0, 1), slab_of(0, 1, 0))
    ylo = (b, slab_of(0, 1, 0))
    back = [(2, 0), (2, 1), (1, 0), (3, 0), (1, 1), (3, 1), (0, 1)]
    back_id = [(blk_of(dz), slab_of(0, 0, dc)) for dz, dc in back]
    plane = [(dh, dx, dl) for dx in (0, 1, 3, 2) for dh in (0, 1) for dl in (0, 1) if (dh, dx, dl) != (0, 0, 0)]
    plane_id = [(blk_of(0, dh), slab_of(dx, dl)) for dh, dx, dl in plane]
    partners = back_id + plane_id

    barrier = pltpu.get_barrier_semaphore()
    for p in partners:
        pl.semaphore_signal(barrier, inc=1, device_id=p, device_id_type=MESH)

    def rows(ref, at, n=CH):
        return ref.at[pl.ds(at, n)]

    loads = [pltpu.make_async_copy(new_hbm, rows(nr, 0, ROWS), load_sem.at[0])]
    half_to = pl.multiple_of((1 - l) * (COMMON // 2), 128)
    half_here = pl.multiple_of(l * (COMMON // 2), 128)
    index_parts = [(pl.multiple_of(COMMON + x * UNIT, 64), UNIT), (half_to, COMMON // 2), (half_here, COMMON // 2)]
    index_parts += [(pl.multiple_of(COMMON + ring4(x + j) * UNIT, 64), UNIT) for j in (1, 2, 3)]
    for j, (at, n) in enumerate(index_parts):
        loads.append(
            pltpu.make_async_copy(
                index_hbm.at[pl.ds(pl.multiple_of(c * HALF + at, 64), n)], rows(ir, at, n), load_sem.at[1 + j]
            )
        )
    small = [
        pltpu.make_async_copy(ref, kept.at[j], load_sem.at[7 + j])
        for j, ref in enumerate((row_hbm, owner_hbm, local_hbm))
    ]
    small.append(pltpu.make_async_copy(pattern_hbm, pattern, load_sem.at[10]))
    for cp in loads + small:
        cp.start()

    def remote(src, dst, ss, rs, dev):
        return pltpu.make_async_remote_copy(
            src_ref=src, dst_ref=dst, send_sem=ss, recv_sem=rs, device_id=dev, device_id_type=MESH
        )

    own_p = [remote(rows(nr, CH * k), rows(nr, quad_at(k)), z_s.at[0, k], z_r.at[0, k], zp) for k in range(4)]
    own_m = [
        remote(rows(nr, CH * ((k + 2) % 4)), rows(nr, quad_at(k) + CH), z_s.at[1, k], z_r.at[1, k], zm)
        for k in range(4)
    ]
    fwd_p = [remote(rows(nr, quad_at(k)), rows(nr, quad_at(4 + k)), z2_s.at[0, k], z2_r.at[0, k], zp) for k in range(2)]
    fwd_m = [
        remote(rows(nr, quad_at(k) + CH), rows(nr, quad_at(4 + k) + CH), z2_s.at[1, k], z2_r.at[1, k], zm)
        for k in range(2)
    ]
    to_sib = [remote(rows(nr, 0, ROWS), rows(nr, ROWS, ROWS), sib_s.at[6], sib_r.at[6], sib)]
    pair_sib = [
        remote(rows(nr, quad_at(k), 2 * CH), rows(nr, quad_at(k) + 2 * CH, 2 * CH), sib_s.at[k], sib_r.at[k], sib)
        for k in range(6)
    ]
    unit_at = [pl.multiple_of(COMMON + x * UNIT + UC * k, 16) for k in (3 * (1 - l), 1, 2, 3 * l)]
    cr = [remote(rows(ir, unit_at[k], UC), rows(oi, CR_AT[k], UC), cr_s.at[k], cr_r.at[k], cross) for k in range(3)]
    yu = [remote(rows(oi, CR_AT[0], UC), rows(oi, CR_AT[3], UC), yu_s.at[0], yu_r.at[0], ylo)]
    common_at = [pl.multiple_of(half_to + CH * k, CH) for k in range(3)]
    ac = [remote(rows(ir, common_at[k]), rows(oi, AC_AT[k]), ac_s.at[k], ac_r.at[k], cross) for k in range(3)]
    ay = [remote(rows(oi, AC_AT[k]), rows(oi, AY_AT[k]), ay_s.at[k], ay_r.at[k], ylo) for k in range(3)]
    x_p = [remote(rows(oi, CR_AT[k], UC), rows(oi, XM_AT[k], UC), x_s.at[0, k], x_r.at[0, k], xp) for k in range(4)]
    x_m = [remote(rows(oi, CR_AT[k], UC), rows(oi, XP_AT[k], UC), x_s.at[1, k], x_r.at[1, k], xm) for k in range(4)]
    x_f = [
        remote(rows(oi, (XP_AT if k % 2 else XM_AT)[k], UC), rows(oi, X2_AT[k], UC), x2_s.at[k], x2_r.at[k], xm if k % 2 else xp)
        for k in range(4)
    ]
    code = [remote(codes.at[0], codes.at[1 + i], code_s.at[i], code_r.at[i], dev) for i, dev in enumerate(back_id)]

    def place_of(dh, dx, dl):
        return (1 - h if dh else h) * 8 + ring4(x + dx) * 2 + (1 - l if dl else l)

    def cluster_rows(dh, dx, dl):
        return pl.ds(pl.multiple_of(place_of(dh, dx, dl) * CL_DEV, CL_DEV), CL_DEV)

    sums = [
        remote(partial.at[cluster_rows(*plane[j])], got.at[j], sum_s.at[j], sum_r.at[j], plane_id[j])
        for j in range(len(plane))
    ]

    lates = [
        remote(late.at[place_of(*plane[j])], late_got.at[j], late_s.at[j], late_r.at[j], plane_id[j])
        for j in range(len(plane))
    ]

    acc0[...] = jnp.full(acc0.shape, -3.0, jnp.float32)
    acc1[...] = jnp.full(acc1.shape, -3.0, jnp.float32)

    def normalize(ref, at, n=CH):
        ref[pl.ds(at, n), :] = unit_rows(ref[pl.ds(at, n), :])

    loads[0].wait()
    normalize(nr, 0)
    normalize(nr, 2 * CH)
    normalize(nr, CH)
    normalize(nr, 3 * CH)
    loads[1].wait()
    for k in range(4):
        normalize(ir, unit_at[k], UC)
    for cp in small:
        cp.wait()
    codes[0] = (kept[1] * CL_DEV + kept[2]) * ROWS + kept[0]
    loads[2].wait()
    for k in range(3):
        normalize(ir, common_at[k])
    def scores(acc, idx, i_at, i_n, n_at, n_n):
        prod = lax.dot_general(
            idx[pl.ds(i_at, i_n), :], nr[pl.ds(n_at, n_n), :],
            (((1,), (1,)), ((), ())), preferred_element_type=jnp.float32,
        )
        top = jnp.max(prod.reshape(i_n // 8, 8, n_n), axis=0)
        acc[:, pl.ds(n_at, n_n)] = jnp.maximum(acc[:, pl.ds(n_at, n_n)], top)

    def own_range(n_at, n_end):
        scores(acc0, ir, 0, HALF, n_at, n_end - n_at)

    def other_range(i_at, i_end, n_at, n_end):
        scores(acc1, oi, i_at, i_end - i_at, n_at, n_end - n_at)

    def z_in(k, side):
        (own_p, own_m)[side][k].wait_recv()
        if k < 2:
            (fwd_p, fwd_m)[side][k].start()

    def cross_in(k):
        (cr + yu)[k].wait_recv()
        if k == 0:
            yu[0].start()
        x_p[k].start()
        x_m[k].start()

    def common_in(k):
        ac[k].wait_recv()
        ay[k].start()

    def x_in(k, side):
        (x_p, x_m)[side][k].wait_recv()
        if k % 2 == side:
            x_f[k].start()

    def hot(count, which):
        at = lax.broadcasted_iota(jnp.int32, (count, KEEP), 0)
        return jnp.where(at == which, 1.0, 0.0).astype(jnp.bfloat16)

    def product(left, right):
        return lax.dot_general(left, right, (((1,), (1,)), ((), ())), preferred_element_type=jnp.float32)

    def weigh(slot, dz, dc):
        both = codes[slot]
        row = lax.rem(both, ROWS)
        local = lax.rem(lax.div(both, ROWS), CL_DEV)
        owner = lax.div(both, ROWS * CL_DEV)
        o_blk, o_slab = lax.div(owner, 16), lax.rem(owner, 16)
        mine = (lax.div(o_blk, 2) == z) & (lax.rem(o_slab, 2) == c)
        place = jnp.where(mine, lax.rem(o_blk, 2) * 8 + lax.div(o_slab, 2), -1)
        named = hot(PLANE, jnp.where(mine, place * CL_DEV + local, -1))
        count = jnp.sum(named.astype(jnp.float32), axis=1, keepdims=True)
        if dz != 2:
            table, width, first = weights, named, 0
        else:
            to = hot(16, place)
            before, after = (lax.broadcasted_iota(jnp.int32, (KEEP, KEEP), axis) for axis in (0, 1))
            sooner = jnp.where(before < after, 1.0, 0.0).astype(jnp.bfloat16)
            sooner = jnp.dot(to, sooner, preferred_element_type=jnp.float32)
            rank = jnp.sum(to.astype(jnp.float32) * sooner, axis=0, keepdims=True).astype(jnp.int32)
            table, first = late_weights, LATE
            width = hot(8 * 16, jnp.where(mine, place * 8 + dc * KCAP + rank, -1))
        spread = product(width, hot(ROWS, row)).astype(jnp.bfloat16)
        for q, at in enumerate(places(dz, dc)):
            table[:, pl.ds(at - first, CH)] = spread[:, CH * q : CH * (q + 1)]
        return count, product(width, hot(128, local)) if dz == 2 else 0.0

    def send_sums():
        partial[...] = jnp.dot(weights[...], nr[pl.ds(0, LATE), :], preferred_element_type=jnp.float32)
        for cp in sums:
            cp.start()

    def send_late():
        picked = jnp.dot(late_weights[...], nr[pl.ds(LATE, 2 * ROWS), :], preferred_element_type=jnp.float32)
        for q in range(16):
            late[q, :, pl.ds(0, D)] = picked[8 * q : 8 * (q + 1)].astype(jnp.bfloat16)
        late_got[15] = late[place_of(0, 0, 0)]
        for cp in lates:
            cp.start()

    def weigh_next(i):
        dz, dc = back[i]
        code[i].wait_recv()
        more, tag = weigh(1 + i, (4 - dz) % 4, dc)
        tally[...] = tally[...] + more
        if dz == 2:
            tags[...] = tags[...] + tag

    def write_tags():
        lane = lax.broadcasted_iota(jnp.int32, (8, 128), 1)
        for q in range(16):
            mixed = tags[pl.ds(8 * q, 8), :]
            for g in range(2):
                mixed = jnp.where(lane == CL_DEV + g, tally[pl.ds(16 * q + 8 * g, 8), :], mixed)
            late[q, :, pl.ds(D, 128)] = mixed.astype(jnp.bfloat16)

    for j in range(2, 6):
        loads[1 + j].wait()
        at, n = index_parts[j]
        step = CH if n % CH == 0 else UC
        for k in range(n // step):
            normalize(ir, pl.multiple_of(at + step * k, 16), step)

    pl.semaphore_wait(barrier, len(partners))
    for cp in code:
        cp.start()
    for k in range(4):
        own_p[k].start()
        own_m[k].start()
    for cp in cr + ac:
        cp.start()
    to_sib[0].start()
    own_range(0, ROWS)
    count, _ = weigh(0, 0, 0)
    tally[...] = jnp.broadcast_to(count, (PLANE, 128))
    tags[...] = jnp.zeros(tags.shape, jnp.float32)
    weigh_next(0)
    weigh_next(1)
    weigh_next(2)
    weigh_next(3)
    weigh_next(4)
    weigh_next(5)
    to_sib[0].wait_recv()
    own_range(512, 1024)
    weigh_next(6)
    write_tags()
    cross_in(0)
    z_in(0, 0)
    z_in(0, 1)
    pair_sib[0].start()
    own_range(1024, 1280)
    cross_in(1)
    pair_sib[0].wait_recv()
    own_range(1280, 1536)
    cross_in(3)
    x_in(0, 0)
    x_in(0, 1)
    cross_in(2)
    other_range(0, 480, 512, 1536)
    z_in(1, 0)
    z_in(1, 1)
    pair_sib[1].start()
    own_range(1536, 1792)
    x_in(1, 0)
    x_in(1, 1)
    pair_sib[1].wait_recv()
    own_range(1792, 2048)
    common_in(0)
    z_in(2, 0)
    z_in(2, 1)
    pair_sib[2].start()
    x_in(3, 0)
    x_in(3, 1)
    other_range(0, 928, 1536, 2304)
    other_range(480, 928, 512, 1536)
    pair_sib[2].wait_recv()
    own_range(2048, 2560)
    x_f[0].wait_recv()
    x_in(2, 1)
    common_in(1)
    z_in(3, 0)
    z_in(3, 1)
    pair_sib[3].start()
    other_range(1008, 1296, 512, 2816)
    x_in(2, 0)
    x_f[1].wait_recv()
    ay[0].wait_recv()
    other_range(0, 928, 2304, 2816)
    pair_sib[3].wait_recv()
    own_range(2560, 3072)
    common_in(2)
    x_f[3].wait_recv()
    fwd_p[0].wait_recv()
    fwd_m[0].wait_recv()
    pair_sib[4].start()
    other_range(0, 1296, 2816, 3328)
    other_range(1456, 1792, 512, 3328)
    x_f[2].wait_recv()
    pair_sib[4].wait_recv()
    ay[1].wait_recv()
    send_sums()
    fwd_p[1].wait_recv()
    fwd_m[1].wait_recv()
    pair_sib[5].start()
    own_range(3072, 3584)
    pair_sib[5].wait_recv()
    send_late()
    ay[2].wait_recv()
    other_range(0, 2048, 3328, 3840)
    own_range(3584, 4096)
    other_range(1792, 2048, 512, 3328)
    other_range(0, 2048, 3840, 4096)
    other_range(1296, 1456, 512, 3328)
    other_range(928, 1008, 512, 2816)

    def block_best(dz, dc):
        row = blk_of(dz) * 16 + slab_of(0, 0, dc)
        live0 = jnp.full((8, CH), pattern[b, row], jnp.int32) > 0
        live1 = jnp.full((8, CH), pattern[blk_of(0, 1), row], jnp.int32) > 0
        parts = []
        for w in places(dz, dc):
            here = jnp.where(live0, acc0[:, pl.ds(w, CH)], -2.0)
            there = jnp.where(live1, acc1[:, pl.ds(w, CH)], -2.0)
            parts.append(jnp.max(jnp.maximum(here, there), axis=0, keepdims=True))
        return jnp.concatenate(parts, axis=1)

    rets = []
    for i, (dz, dc) in enumerate(back):
        ret_out[i] = block_best(dz, dc)
        cp = remote(ret_out.at[i], ret_in.at[i], ret_s.at[i], ret_r.at[i], back_id[i])
        cp.start()
        rets.append(cp)
    other_range(0, HALF, 0, 512)
    best = block_best(0, 0)
    total = partial[cluster_rows(0, 0, 0), :]
    for j, cp in enumerate(sums):
        cp.wait_recv()
        total = total + got[j]
    for cp in lates:
        cp.wait_recv()
    slots = late_got[...].astype(jnp.float32).reshape(16 * 8, WIDE)
    clusters = slots[:, D:].T.astype(jnp.bfloat16)
    last = jnp.dot(clusters, slots[:, :D].astype(jnp.bfloat16), preferred_element_type=jnp.float32)
    sums_ref[...] = total + last[:CL_DEV]
    counts_ref[...] = jnp.sum(late_got[:, :, pl.ds(D, 128)].astype(jnp.float32), axis=0)
    for i, cp in enumerate(rets):
        cp.wait_recv()
        best = jnp.maximum(best, ret_in[i])
    best_ref[...] = best
    for cp in own_p + own_m + fwd_p + fwd_m + to_sib + pair_sib + cr + yu + ac + ay + x_p + x_m + x_f + code + sums + lates + rets:
        cp.wait_send()


def parted(best_in, sums_in, counts_in, best_ref, sums_ref, counts_ref):
    best_ref[...] = best_in[...]
    sums_ref[...] = sums_in[...]
    row, lane = (lax.broadcasted_iota(jnp.int32, (8, 128), axis) for axis in (0, 1))
    counts = 0.0
    for g in range(2):
        column = counts_in[:, CL_DEV + g : CL_DEV + g + 1]
        counts = counts + jnp.where(lane == row + 8 * g, column, 0.0)
    counts_ref[...] = jnp.sum(counts, axis=0, keepdims=True)[:, :CL_DEV]


def per_device(new_rows, index_rows, pattern, kept_row, kept_owner, kept_local):
    dma = pltpu.SemaphoreType.DMA
    f32, bf16, i32 = jnp.float32, jnp.bfloat16, jnp.int32
    best, sums, counts = pl.pallas_call(
        window_kernel,
        out_shape=(
            jax.ShapeDtypeStruct((1, ROWS), f32),
            jax.ShapeDtypeStruct((CL_DEV, D), f32),
            jax.ShapeDtypeStruct((8, 128), f32),
        ),
        in_specs=[pl.BlockSpec(memory_space=pl.ANY)] * 6,
        out_specs=[pl.BlockSpec(memory_space=pltpu.VMEM)] * 3,
        scratch_shapes=[
            pltpu.VMEM((8 * ROWS, D), bf16),
            pltpu.VMEM((HALF, D), bf16),
            pltpu.VMEM((HALF, D), bf16),
            pltpu.VMEM((8, 8 * ROWS), f32),
            pltpu.VMEM((8, 8 * ROWS), f32),
            pltpu.VMEM((7, 1, ROWS), f32),
            pltpu.VMEM((7, 1, ROWS), f32),
            pltpu.SMEM((8, 128), i32),
            pltpu.VMEM((3, 1, KEEP), i32),
            pltpu.VMEM((8, 1, KEEP), i32),
            pltpu.VMEM((PLANE, LATE), bf16),
            pltpu.VMEM((PLANE, D), f32),
            pltpu.VMEM((15, CL_DEV, D), f32),
            pltpu.VMEM((8 * 16, 2 * ROWS), bf16),
            pltpu.VMEM((16, 8, WIDE), bf16),
            pltpu.VMEM((16, 8, WIDE), bf16),
            pltpu.VMEM((8 * 16, 128), f32),
            pltpu.VMEM((PLANE, 128), f32),
            dma((11,)),
            dma((2, 4)), dma((2, 4)), dma((2, 2)), dma((2, 2)), dma((7,)), dma((7,)), dma((4,)), dma((4,)),
            dma((1,)), dma((1,)), dma((3,)), dma((3,)), dma((3,)), dma((3,)),
            dma((2, 4)), dma((2, 4)), dma((4,)), dma((4,)), dma((7,)), dma((7,)), dma((7,)), dma((7,)),
            dma((15,)), dma((15,)), dma((15,)), dma((15,)),
        ],
        compiler_params=pltpu.CompilerParams(
            collective_id=0, has_side_effects=True, vmem_limit_bytes=56 << 20
        ),
        cost_estimate=pl.CostEstimate(flops=2 * 8 * 512 * 4096 * 768, bytes_accessed=10 << 20, transcendentals=0),
    )(
        new_rows,
        index_rows,
        pattern.T,
        kept_row.reshape(1, KEEP),
        kept_owner.reshape(1, KEEP),
        kept_local.reshape(1, KEEP),
    )
    best, sums, counts = pl.pallas_call(
        parted,
        out_shape=(
            jax.ShapeDtypeStruct((1, ROWS), f32),
            jax.ShapeDtypeStruct((CL_DEV, D), f32),
            jax.ShapeDtypeStruct((1, CL_DEV), f32),
        ),
        in_specs=[pl.BlockSpec(memory_space=pltpu.VMEM)] * 3,
        out_specs=[pl.BlockSpec(memory_space=pltpu.VMEM)] * 3,
    )(best, sums, counts)
    return (best.reshape(ROWS), sums, counts.reshape(CL_DEV))


def solution(mesh):
    placed = (
        P(("blk", "slab"), None),
        P("blk", None),
        P(),
        P(("blk", "slab")),
        P(("blk", "slab"), None),
        P(("blk", "slab")),
    )
    return jax.shard_map(
        per_device,
        mesh=mesh,
        in_specs=placed,
        out_specs=(P(("blk", "slab")), P(("blk", "slab"), None), P(("blk", "slab"))),
        check_vma=False,
    )
```

```python
import jax
import jax.numpy as jnp
from jax import lax
from jax.experimental import pallas as pl
from jax.experimental.pallas import tpu as pltpu
from jax.sharding import PartitionSpec as P

CL_DEV = 16
EPS = 1e-06
MESH = pl.DeviceIdType.MESH
ROWS = 512
KEEP = 256
CH = 128
D = 768
HALF = 2048
UC = 80
UNIT = 4 * UC
COMMON = 768
WIDE = D + 128
KCAP = 4
LATE = 3072
PLANE = 256


def unit_rows(values):
    wide = values.astype(jnp.float32)
    scale = lax.rsqrt(jnp.sum(wide * wide, axis=-1, keepdims=True) + EPS)
    return (wide * scale).astype(jnp.bfloat16)


def ring4(v):
    return lax.rem(v + 4, 4)


def quad_at(k):
    return 2 * ROWS + ROWS * k


def places(dz, dc):
    side = 2 * CH * dc
    if dz == 0:
        return [ROWS * dc + CH * q for q in range(4)]
    if dz == 3:
        return [quad_at(q) + side for q in range(4)]
    if dz == 1:
        return [quad_at((q + 2) % 4) + side + CH for q in range(4)]
    return [quad_at(4 + q % 2) + side + CH * (q // 2) for q in range(4)]


CR_AT = (0, UC, 2 * UC, 3 * UC)
XM_AT = (320, 480, 928, 640)
XP_AT = (400, 560, 1008, 720)
AC_AT = (800, 1088, 1536)
X2_AT = (1216, 1296, 1376, 1456)
AY_AT = (1664, 1792, 1920)


def window_kernel(
    new_hbm, index_hbm, pattern_hbm, row_hbm, owner_hbm, local_hbm, best_ref, sums_ref, counts_ref,
    nr, ir, oi, acc0, acc1, ret_out, ret_in, pattern, kept, codes, weights, partial, got,
    late_weights, late, late_got, tags, tally,
    load_sem, z_s, z_r, z2_s, z2_r, sib_s, sib_r, cr_s, cr_r, yu_s, yu_r, ac_s, ac_r, ay_s, ay_r,
    x_s, x_r, x2_s, x2_r, ret_s, ret_r, code_s, code_r, sum_s, sum_r, late_s, late_r,
):
    b = lax.axis_index("blk")
    s = lax.axis_index("slab")
    z, h = lax.div(b, 2), lax.rem(b, 2)
    x, l, c = lax.div(s, 4), lax.rem(lax.div(s, 2), 2), lax.rem(s, 2)

    def blk_of(dz, dh=0):
        return ring4(z + dz) * 2 + (1 - h if dh else h)

    def slab_of(dx=0, dl=0, dc=0):
        return (ring4(x + dx) * 2 + (1 - l if dl else l)) * 2 + (1 - c if dc else c)

    zp, zm = (blk_of(1), s), (blk_of(-1), s)
    xp, xm = (b, slab_of(1)), (b, slab_of(-1))
    sib = (b, slab_of(0, 0, 1))
    cross = (blk_of(0, 1), slab_of(0, 1, 0))
    ylo = (b, slab_of(0, 1, 0))
    back = [(2, 0), (2, 1), (1, 0), (3, 0), (1, 1), (3, 1), (0, 1)]
    back_id = [(blk_of(dz), slab_of(0, 0, dc)) for dz, dc in back]
    plane = [(dh, dx, dl) for dx in (0, 1, 3, 2) for dh in (0, 1) for dl in (0, 1) if (dh, dx, dl) != (0, 0, 0)]
    plane_id = [(blk_of(0, dh), slab_of(dx, dl)) for dh, dx, dl in plane]
    partners = back_id + plane_id

    barrier = pltpu.get_barrier_semaphore()
    for p in partners:
        pl.semaphore_signal(barrier, inc=1, device_id=p, device_id_type=MESH)

    def rows(ref, at, n=CH):
        return ref.at[pl.ds(at, n)]

    loads = [pltpu.make_async_copy(new_hbm, rows(nr, 0, ROWS), load_sem.at[0])]
    half_to = pl.multiple_of((1 - l) * (COMMON // 2), 128)
    half_here = pl.multiple_of(l * (COMMON // 2), 128)
    index_parts = [(pl.multiple_of(COMMON + x * UNIT, 64), UNIT), (half_to, COMMON // 2), (half_here, COMMON // 2)]
    index_parts += [(pl.multiple_of(COMMON + ring4(x + j) * UNIT, 64), UNIT) for j in (1, 2, 3)]
    for j, (at, n) in enumerate(index_parts):
        loads.append(
            pltpu.make_async_copy(
                index_hbm.at[pl.ds(pl.multiple_of(c * HALF + at, 64), n)], rows(ir, at, n), load_sem.at[1 + j]
            )
        )
    small = [
        pltpu.make_async_copy(ref, kept.at[j], load_sem.at[7 + j])
        for j, ref in enumerate((row_hbm, owner_hbm, local_hbm))
    ]
    small.append(pltpu.make_async_copy(pattern_hbm, pattern, load_sem.at[10]))
    for cp in loads + small:
        cp.start()

    def remote(src, dst, ss, rs, dev):
        return pltpu.make_async_remote_copy(
            src_ref=src, dst_ref=dst, send_sem=ss, recv_sem=rs, device_id=dev, device_id_type=MESH
        )

    own_p = [remote(rows(nr, CH * k), rows(nr, quad_at(k)), z_s.at[0, k], z_r.at[0, k], zp) for k in range(4)]
    own_m = [
        remote(rows(nr, CH * ((k + 2) % 4)), rows(nr, quad_at(k) + CH), z_s.at[1, k], z_r.at[1, k], zm)
        for k in range(4)
    ]
    fwd_p = [remote(rows(nr, quad_at(k)), rows(nr, quad_at(4 + k)), z2_s.at[0, k], z2_r.at[0, k], zp) for k in range(2)]
    fwd_m = [
        remote(rows(nr, quad_at(k) + CH), rows(nr, quad_at(4 + k) + CH), z2_s.at[1, k], z2_r.at[1, k], zm)
        for k in range(2)
    ]
    to_sib = [remote(rows(nr, 0, ROWS), rows(nr, ROWS, ROWS), sib_s.at[6], sib_r.at[6], sib)]
    pair_sib = [
        remote(rows(nr, quad_at(k), 2 * CH), rows(nr, quad_at(k) + 2 * CH, 2 * CH), sib_s.at[k], sib_r.at[k], sib)
        for k in range(6)
    ]
    unit_at = [pl.multiple_of(COMMON + x * UNIT + UC * k, 16) for k in (3 * (1 - l), 1, 2, 3 * l)]
    cr = [remote(rows(ir, unit_at[k], UC), rows(oi, CR_AT[k], UC), cr_s.at[k], cr_r.at[k], cross) for k in range(3)]
    yu = [remote(rows(oi, CR_AT[0], UC), rows(oi, CR_AT[3], UC), yu_s.at[0], yu_r.at[0], ylo)]
    common_at = [pl.multiple_of(half_to + CH * k, CH) for k in range(3)]
    ac = [remote(rows(ir, common_at[k]), rows(oi, AC_AT[k]), ac_s.at[k], ac_r.at[k], cross) for k in range(3)]
    ay = [remote(rows(oi, AC_AT[k]), rows(oi, AY_AT[k]), ay_s.at[k], ay_r.at[k], ylo) for k in range(3)]
    x_p = [remote(rows(oi, CR_AT[k], UC), rows(oi, XM_AT[k], UC), x_s.at[0, k], x_r.at[0, k], xp) for k in range(4)]
    x_m = [remote(rows(oi, CR_AT[k], UC), rows(oi, XP_AT[k], UC), x_s.at[1, k], x_r.at[1, k], xm) for k in range(4)]
    x_f = [
        remote(rows(oi, (XP_AT if k % 2 else XM_AT)[k], UC), rows(oi, X2_AT[k], UC), x2_s.at[k], x2_r.at[k], xm if k % 2 else xp)
        for k in range(4)
    ]
    code = [remote(codes.at[0], codes.at[1 + i], code_s.at[i], code_r.at[i], dev) for i, dev in enumerate(back_id)]

    def place_of(dh, dx, dl):
        return (1 - h if dh else h) * 8 + ring4(x + dx) * 2 + (1 - l if dl else l)

    def cluster_rows(dh, dx, dl):
        return pl.ds(pl.multiple_of(place_of(dh, dx, dl) * CL_DEV, CL_DEV), CL_DEV)

    sums = [
        remote(partial.at[cluster_rows(*plane[j])], got.at[j], sum_s.at[j], sum_r.at[j], plane_id[j])
        for j in range(len(plane))
    ]

    lates = [
        remote(late.at[place_of(*plane[j])], late_got.at[j], late_s.at[j], late_r.at[j], plane_id[j])
        for j in range(len(plane))
    ]

    acc0[...] = jnp.full(acc0.shape, -3.0, jnp.float32)
    acc1[...] = jnp.full(acc1.shape, -3.0, jnp.float32)

    def normalize(ref, at, n=CH):
        ref[pl.ds(at, n), :] = unit_rows(ref[pl.ds(at, n), :])

    loads[0].wait()
    normalize(nr, 0)
    normalize(nr, 2 * CH)
    normalize(nr, CH)
    normalize(nr, 3 * CH)
    loads[1].wait()
    for k in range(4):
        normalize(ir, unit_at[k], UC)
    for cp in small:
        cp.wait()
    codes[0] = (kept[1] * CL_DEV + kept[2]) * ROWS + kept[0]
    loads[2].wait()
    for k in range(3):
        normalize(ir, common_at[k])
    def scores(acc, idx, i_at, i_n, n_at, n_n):
        prod = lax.dot_general(
            idx[pl.ds(i_at, i_n), :], nr[pl.ds(n_at, n_n), :],
            (((1,), (1,)), ((), ())), preferred_element_type=jnp.float32,
        )
        top = jnp.max(prod.reshape(i_n // 8, 8, n_n), axis=0)
        acc[:, pl.ds(n_at, n_n)] = jnp.maximum(acc[:, pl.ds(n_at, n_n)], top)

    def own_range(n_at, n_end):
        scores(acc0, ir, 0, HALF, n_at, n_end - n_at)

    def other_range(i_at, i_end, n_at, n_end):
        scores(acc1, oi, i_at, i_end - i_at, n_at, n_end - n_at)

    def z_in(k, side):
        (own_p, own_m)[side][k].wait_recv()
        if k < 2:
            (fwd_p, fwd_m)[side][k].start()

    def cross_in(k):
        (cr + yu)[k].wait_recv()
        if k == 0:
            yu[0].start()
        x_p[k].start()
        x_m[k].start()

    def common_in(k):
        ac[k].wait_recv()
        ay[k].start()

    def x_in(k, side):
        (x_p, x_m)[side][k].wait_recv()
        if k % 2 == side:
            x_f[k].start()

    def hot(count, which):
        at = lax.broadcasted_iota(jnp.int32, (count, KEEP), 0)
        return jnp.where(at == which, 1.0, 0.0).astype(jnp.bfloat16)

    def product(left, right):
        return lax.dot_general(left, right, (((1,), (1,)), ((), ())), preferred_element_type=jnp.float32)

    def weigh(slot, dz, dc):
        both = codes[slot]
        row = lax.rem(both, ROWS)
        local = lax.rem(lax.div(both, ROWS), CL_DEV)
        owner = lax.div(both, ROWS * CL_DEV)
        o_blk, o_slab = lax.div(owner, 16), lax.rem(owner, 16)
        mine = (lax.div(o_blk, 2) == z) & (lax.rem(o_slab, 2) == c)
        place = jnp.where(mine, lax.rem(o_blk, 2) * 8 + lax.div(o_slab, 2), -1)
        named = hot(PLANE, jnp.where(mine, place * CL_DEV + local, -1))
        count = jnp.sum(named.astype(jnp.float32), axis=1, keepdims=True)
        if dz != 2:
            table, width, first = weights, named, 0
        else:
            to = hot(16, place)
            before, after = (lax.broadcasted_iota(jnp.int32, (KEEP, KEEP), axis) for axis in (0, 1))
            sooner = jnp.where(before < after, 1.0, 0.0).astype(jnp.bfloat16)
            sooner = jnp.dot(to, sooner, preferred_element_type=jnp.float32)
            rank = jnp.sum(to.astype(jnp.float32) * sooner, axis=0, keepdims=True).astype(jnp.int32)
            table, first = late_weights, LATE
            width = hot(8 * 16, jnp.where(mine, place * 8 + dc * KCAP + rank, -1))
        spread = product(width, hot(ROWS, row)).astype(jnp.bfloat16)
        for q, at in enumerate(places(dz, dc)):
            table[:, pl.ds(at - first, CH)] = spread[:, CH * q : CH * (q + 1)]
        return count, product(width, hot(128, local)) if dz == 2 else 0.0

    def send_sums():
        partial[...] = jnp.dot(weights[...], nr[pl.ds(0, LATE), :], preferred_element_type=jnp.float32)
        for cp in sums:
            cp.start()

    def send_late():
        picked = jnp.dot(late_weights[...], nr[pl.ds(LATE, 2 * ROWS), :], preferred_element_type=jnp.float32)
        for q in range(16):
            late[q, :, pl.ds(0, D)] = picked[8 * q : 8 * (q + 1)].astype(jnp.bfloat16)
        late_got[15] = late[place_of(0, 0, 0)]
        for cp in lates:
            cp.start()

    def weigh_next(i):
        dz, dc = back[i]
        code[i].wait_recv()
        more, tag = weigh(1 + i, (4 - dz) % 4, dc)
        tally[...] = tally[...] + more
        if dz == 2:
            tags[...] = tags[...] + tag

    def write_tags():
        lane = lax.broadcasted_iota(jnp.int32, (8, 128), 1)
        for q in range(16):
            mixed = tags[pl.ds(8 * q, 8), :]
            for g in range(2):
                mixed = jnp.where(lane == CL_DEV + g, tally[pl.ds(16 * q + 8 * g, 8), :], mixed)
            late[q, :, pl.ds(D, 128)] = mixed.astype(jnp.bfloat16)

    pl.semaphore_wait(barrier, len(partners))
    for cp in code:
        cp.start()
    for k in range(4):
        own_p[k].start()
        own_m[k].start()
    for cp in cr + ac:
        cp.start()
    to_sib[0].start()
    for j in range(2, 6):
        loads[1 + j].wait()
        at, n = index_parts[j]
        step = CH if n % CH == 0 else UC
        for k in range(n // step):
            normalize(ir, pl.multiple_of(at + step * k, 16), step)

    own_range(0, ROWS)
    count, _ = weigh(0, 0, 0)
    tally[...] = jnp.broadcast_to(count, (PLANE, 128))
    tags[...] = jnp.zeros(tags.shape, jnp.float32)
    weigh_next(0)
    weigh_next(1)
    weigh_next(2)
    weigh_next(3)
    weigh_next(4)
    weigh_next(5)
    to_sib[0].wait_recv()
    own_range(512, 1024)
    weigh_next(6)
    write_tags()
    cross_in(0)
    z_in(0, 0)
    z_in(0, 1)
    pair_sib[0].start()
    own_range(1024, 1280)
    cross_in(1)
    pair_sib[0].wait_recv()
    own_range(1280, 1536)
    cross_in(3)
    x_in(0, 0)
    x_in(0, 1)
    cross_in(2)
    other_range(0, 480, 512, 1536)
    z_in(1, 0)
    z_in(1, 1)
    pair_sib[1].start()
    own_range(1536, 1792)
    x_in(1, 0)
    x_in(1, 1)
    pair_sib[1].wait_recv()
    own_range(1792, 2048)
    common_in(0)
    z_in(2, 0)
    z_in(2, 1)
    pair_sib[2].start()
    x_in(3, 0)
    x_in(3, 1)
    other_range(0, 928, 1536, 2304)
    other_range(480, 928, 512, 1536)
    pair_sib[2].wait_recv()
    own_range(2048, 2560)
    x_f[0].wait_recv()
    x_in(2, 1)
    common_in(1)
    z_in(3, 0)
    z_in(3, 1)
    pair_sib[3].start()
    other_range(1008, 1296, 512, 2816)
    x_in(2, 0)
    x_f[1].wait_recv()
    ay[0].wait_recv()
    other_range(0, 928, 2304, 2816)
    pair_sib[3].wait_recv()
    own_range(2560, 3072)
    common_in(2)
    x_f[3].wait_recv()
    fwd_p[0].wait_recv()
    fwd_m[0].wait_recv()
    pair_sib[4].start()
    other_range(0, 1296, 2816, 3328)
    other_range(1456, 1792, 512, 3328)
    x_f[2].wait_recv()
    pair_sib[4].wait_recv()
    ay[1].wait_recv()
    send_sums()
    fwd_p[1].wait_recv()
    fwd_m[1].wait_recv()
    pair_sib[5].start()
    own_range(3072, 3584)
    pair_sib[5].wait_recv()
    send_late()
    ay[2].wait_recv()
    other_range(0, 2048, 3328, 3840)
    own_range(3584, 4096)
    other_range(1792, 2048, 512, 3328)
    other_range(0, 2048, 3840, 4096)
    other_range(1296, 1456, 512, 3328)
    other_range(928, 1008, 512, 2816)

    def block_best(dz, dc):
        row = blk_of(dz) * 16 + slab_of(0, 0, dc)
        live0 = jnp.full((8, CH), pattern[b, row], jnp.int32) > 0
        live1 = jnp.full((8, CH), pattern[blk_of(0, 1), row], jnp.int32) > 0
        parts = []
        for w in places(dz, dc):
            here = jnp.where(live0, acc0[:, pl.ds(w, CH)], -2.0)
            there = jnp.where(live1, acc1[:, pl.ds(w, CH)], -2.0)
            parts.append(jnp.max(jnp.maximum(here, there), axis=0, keepdims=True))
        return jnp.concatenate(parts, axis=1)

    rets = []
    for i, (dz, dc) in enumerate(back):
        ret_out[i] = block_best(dz, dc)
        cp = remote(ret_out.at[i], ret_in.at[i], ret_s.at[i], ret_r.at[i], back_id[i])
        cp.start()
        rets.append(cp)
    other_range(0, HALF, 0, 512)
    best = block_best(0, 0)
    total = partial[cluster_rows(0, 0, 0), :]
    for j, cp in enumerate(sums):
        cp.wait_recv()
        total = total + got[j]
    for cp in lates:
        cp.wait_recv()
    slots = late_got[...].astype(jnp.float32).reshape(16 * 8, WIDE)
    clusters = slots[:, D:].T.astype(jnp.bfloat16)
    last = jnp.dot(clusters, slots[:, :D].astype(jnp.bfloat16), preferred_element_type=jnp.float32)
    sums_ref[...] = total + last[:CL_DEV]
    counts_ref[...] = jnp.sum(late_got[:, :, pl.ds(D, 128)].astype(jnp.float32), axis=0)
    for i, cp in enumerate(rets):
        cp.wait_recv()
        best = jnp.maximum(best, ret_in[i])
    best_ref[...] = best
    for cp in own_p + own_m + fwd_p + fwd_m + to_sib + pair_sib + cr + yu + ac + ay + x_p + x_m + x_f + code + sums + lates + rets:
        cp.wait_send()


def parted(best_in, sums_in, counts_in, best_ref, sums_ref, counts_ref):
    best_ref[...] = best_in[...]
    sums_ref[...] = sums_in[...]
    row, lane = (lax.broadcasted_iota(jnp.int32, (8, 128), axis) for axis in (0, 1))
    counts = 0.0
    for g in range(2):
        column = counts_in[:, CL_DEV + g : CL_DEV + g + 1]
        counts = counts + jnp.where(lane == row + 8 * g, column, 0.0)
    counts_ref[...] = jnp.sum(counts, axis=0, keepdims=True)[:, :CL_DEV]


def per_device(new_rows, index_rows, pattern, kept_row, kept_owner, kept_local):
    dma = pltpu.SemaphoreType.DMA
    f32, bf16, i32 = jnp.float32, jnp.bfloat16, jnp.int32
    best, sums, counts = pl.pallas_call(
        window_kernel,
        out_shape=(
            jax.ShapeDtypeStruct((1, ROWS), f32),
            jax.ShapeDtypeStruct((CL_DEV, D), f32),
            jax.ShapeDtypeStruct((8, 128), f32),
        ),
        in_specs=[pl.BlockSpec(memory_space=pl.ANY)] * 6,
        out_specs=[pl.BlockSpec(memory_space=pltpu.VMEM)] * 3,
        scratch_shapes=[
            pltpu.VMEM((8 * ROWS, D), bf16),
            pltpu.VMEM((HALF, D), bf16),
            pltpu.VMEM((HALF, D), bf16),
            pltpu.VMEM((8, 8 * ROWS), f32),
            pltpu.VMEM((8, 8 * ROWS), f32),
            pltpu.VMEM((7, 1, ROWS), f32),
            pltpu.VMEM((7, 1, ROWS), f32),
            pltpu.SMEM((8, 128), i32),
            pltpu.VMEM((3, 1, KEEP), i32),
            pltpu.VMEM((8, 1, KEEP), i32),
            pltpu.VMEM((PLANE, LATE), bf16),
            pltpu.VMEM((PLANE, D), f32),
            pltpu.VMEM((15, CL_DEV, D), f32),
            pltpu.VMEM((8 * 16, 2 * ROWS), bf16),
            pltpu.VMEM((16, 8, WIDE), bf16),
            pltpu.VMEM((16, 8, WIDE), bf16),
            pltpu.VMEM((8 * 16, 128), f32),
            pltpu.VMEM((PLANE, 128), f32),
            dma((11,)),
            dma((2, 4)), dma((2, 4)), dma((2, 2)), dma((2, 2)), dma((7,)), dma((7,)), dma((4,)), dma((4,)),
            dma((1,)), dma((1,)), dma((3,)), dma((3,)), dma((3,)), dma((3,)),
            dma((2, 4)), dma((2, 4)), dma((4,)), dma((4,)), dma((7,)), dma((7,)), dma((7,)), dma((7,)),
            dma((15,)), dma((15,)), dma((15,)), dma((15,)),
        ],
        compiler_params=pltpu.CompilerParams(
            collective_id=0, has_side_effects=True, vmem_limit_bytes=56 << 20
        ),
        cost_estimate=pl.CostEstimate(flops=2 * 8 * 512 * 4096 * 768, bytes_accessed=10 << 20, transcendentals=0),
    )(
        new_rows,
        index_rows,
        pattern.T,
        kept_row.reshape(1, KEEP),
        kept_owner.reshape(1, KEEP),
        kept_local.reshape(1, KEEP),
    )
    best, sums, counts = pl.pallas_call(
        parted,
        out_shape=(
            jax.ShapeDtypeStruct((1, ROWS), f32),
            jax.ShapeDtypeStruct((CL_DEV, D), f32),
            jax.ShapeDtypeStruct((1, CL_DEV), f32),
        ),
        in_specs=[pl.BlockSpec(memory_space=pltpu.VMEM)] * 3,
        out_specs=[pl.BlockSpec(memory_space=pltpu.VMEM)] * 3,
    )(best, sums, counts)
    return (best.reshape(ROWS), sums, counts.reshape(CL_DEV))


def solution(mesh):
    placed = (
        P(("blk", "slab"), None),
        P("blk", None),
        P(),
        P(("blk", "slab")),
        P(("blk", "slab"), None),
        P(("blk", "slab")),
    )
    return jax.shard_map(
        per_device,
        mesh=mesh,
        in_specs=placed,
        out_specs=(P(("blk", "slab")), P(("blk", "slab"), None), P(("blk", "slab"))),
        check_vma=False,
    )
```
